256 devices in a mesh: section: 4 (over x_hi, core), fsdp: 64 (over z, x_lo, y).
Axes of the slice: x: 4 (x_hi: 2, x_lo: 2; x = x_hi * 2 + x_lo), y: 4, z: 8, core: 2. Of those that a mesh axis runs over, the one named last changes fastest.
Arguments:
- signals: bfloat16 [16384, 1536], P('fsdp', 'section'), may hold values from -6 to 6
- conv_weight: bfloat16 [768, 9, 1536], P('fsdp', None, 'section'), may hold values from -0.078125 to 0.078125
- buckets: int32 [2, 2], replicated, may hold values from 0 to 8, as said below
Outputs:
- results: bfloat16 [16384, 1536], P('fsdp', 'section')
- grad_weight: float32 [768, 9, 1536], P('fsdp', None, 'section')
The draws below stay inside these ranges and needn't reach their ends.
Inputs may be any that keep to these rules, and one draw needn't show every extreme that they name: `buckets`: a bucket b means 16 + 2 b live pixels along that side, in the top left of each sample's grid; microbatch 0 has a height bucket of 5 or more; some entry is 8.
All inputs are finite; a program needn't handle non-finite values.
Results may differ from the reference program's by a relative error of at most 0.0054.
Values may be sent and summed in bfloat16 or wider, within the bound.
No kernel may reach another device: no remote copies, remote signals or barrier semaphores. Data moves between devices by JAX's collectives and lax.ppermute only.
A program may use at most 128 MiB of HBM per device.

```python
import jax
import jax.numpy as jnp
from jax import lax

C = 768
GROUPS = 32
SIDE = 32
MICRO = 2
TOK_DEV = 256
TOKENS = 16384


def draw_buckets(key, part):
    base = jax.random.fold_in(key, 7)
    key_h, key_first, key_w, key_forced = jax.random.split(base, 4)
    heights = jax.random.randint(key_h, (MICRO,), 0, 9).astype(jnp.int32)
    first_height = jax.random.randint(key_first, (MICRO,), 5, 9).astype(jnp.int32)
    heights = jnp.where(jnp.arange(MICRO) == 0, first_height, heights)
    widths = jax.random.randint(key_w, (MICRO,), 0, 9).astype(jnp.int32)
    table = jnp.stack([heights, widths], axis=1).reshape(2 * MICRO)
    forced = jax.random.randint(key_forced, (1,), 0, 2 * MICRO).astype(jnp.int32)
    table = jnp.where(jnp.arange(2 * MICRO) == forced[0], jnp.full((2 * MICRO,), 8, jnp.int32), table)
    return table.reshape(MICRO, 2).astype(jnp.int32)


def block_scale(key, shape, cuts, least, largest):
    level, own = 1.0, jax.random.fold_in(key, 6)
    for axis_at, shards_of in cuts:
        steps = jnp.exp(jax.random.uniform(jax.random.fold_in(own, axis_at), (shards_of,), jnp.float32, least / len(cuts), largest / len(cuts)))
        level = level * jnp.repeat(steps, shape[axis_at] // shards_of).reshape([-1 if axis == axis_at else 1 for axis in range(len(shape))])
    return level


def normal_values(own_key, extent, scale, bound, cuts=(), dtype=jnp.bfloat16):
    loudness = block_scale(own_key, extent, cuts, -0.22, 0.18) if cuts else 1.0
    result = jax.random.normal(own_key, extent, jnp.float32) * scale * loudness
    return jnp.minimum(jnp.maximum(result, -bound), bound).astype(dtype)


def setup_inputs(seed: int = 0) -> dict:
    splits = jax.random.split(jax.random.key(seed), 4)
    signals = normal_values(splits[0], (TOKENS, 2 * C), 1.0, 6.0, ((0, 64), (1, 4)))
    conv_weight = normal_values(splits[1], (C, 9, 2 * C), (9 * C) ** -0.5, 0.078125, ((0, 64), (2, 4)))
    buckets = draw_buckets(jax.random.fold_in(splits[3], 71), 0)
    return dict(signals=signals, conv_weight=conv_weight, buckets=buckets)


eps = 1e-05

def silu_slope(value):
    sig = jax.nn.sigmoid(value)
    return sig * (1.0 + value * (1.0 - sig))

def group_view(values):
    return values.reshape(values.shape[0], SIDE, SIDE, GROUPS, C // GROUPS)

def pad_grid(field):
    return jnp.pad(field, ((0, 0), (1, 1), (1, 1), (0, 0)))

def convolve(padded, weight):
    samples = padded.shape[0]
    total = jnp.zeros((samples * SIDE * SIDE, weight.shape[-1]), jnp.float32)
    for tap in range(9):
        row_off, col_off = (tap // 3, tap % 3)
        slab = padded[:, row_off:row_off + SIDE, col_off:col_off + SIDE, :].reshape(-1, padded.shape[-1])
        total = total + jnp.dot(slab, weight[:, tap, :], preferred_element_type=jnp.float32)
    return total.reshape(samples, SIDE, SIDE, -1)

def convolve_back(padded, weight):
    samples = padded.shape[0]
    total = jnp.zeros((samples * SIDE * SIDE, weight.shape[0]), jnp.float32)
    for tap in range(9):
        row_off, col_off = (tap // 3, tap % 3)
        slab = padded[:, 2 - row_off:2 - row_off + SIDE, 2 - col_off:2 - col_off + SIDE, :].reshape(-1, padded.shape[-1])
        total = total + lax.dot_general(slab, weight[:, tap, :], (((1,), (1,)), ((), ())), preferred_element_type=jnp.float32)
    return total.reshape(samples, SIDE, SIDE, -1)

def weight_slope(padded, slope):
    flat = slope.reshape(-1, slope.shape[-1])
    taps = []
    for tap in range(9):
        row_off, col_off = (tap // 3, tap % 3)
        slab = padded[:, row_off:row_off + SIDE, col_off:col_off + SIDE, :].reshape(-1, padded.shape[-1])
        taps.append(lax.dot_general(slab, flat, (((0,), (0,)), ((), ())), preferred_element_type=jnp.float32))
    return jnp.stack(taps, axis=1)

def normalize(values, mask, count):
    grouped = group_view(values * mask)
    kcount = (count * (C // GROUPS))[:, None]
    mean = lax.optimization_barrier(jnp.sum(grouped, axis=(1, 2, 4))) / kcount
    spread = lax.optimization_barrier(jnp.sum(grouped * grouped, axis=(1, 2, 4))) / kcount - mean * mean
    scale = lax.rsqrt(spread + eps)
    normed = (group_view(values) - mean[:, None, None, :, None]) * scale[:, None, None, :, None]
    return (normed.reshape(values.shape), scale)

def block_forward(inputs, weight, mask, count):
    values = inputs.astype(jnp.float32)
    normed, scale = normalize(values, mask, count)
    activated = (mask * jax.nn.silu(normed)).astype(jnp.bfloat16)
    padded = pad_grid(activated)
    mixed = convolve(padded, weight)
    output = (values + mask * mixed).astype(jnp.bfloat16)
    return (output, (normed, scale, padded))

def block_backward(grads, cache, weight, mask, count):
    normed, scale, padded = cache
    slope = (grads.astype(jnp.float32) * mask).astype(jnp.bfloat16)
    slope_pad = pad_grid(slope)
    half = C // 2
    upstream = jnp.zeros(normed.shape, jnp.float32)
    for part in range(2):
        partial_value = convolve_back(slope_pad[..., part * half:(part + 1) * half], weight[:, :, part * half:(part + 1) * half])
        upstream = upstream + lax.optimization_barrier(partial_value.astype(jnp.bfloat16)).astype(jnp.float32)
    gated = mask * upstream * silu_slope(normed)
    grouped = group_view(gated)
    normed_grouped = group_view(normed)
    kcount = (count * (C // GROUPS))[:, None]
    first = lax.optimization_barrier(jnp.sum(grouped, axis=(1, 2, 4))) / kcount
    second = lax.optimization_barrier(jnp.sum(grouped * normed_grouped, axis=(1, 2, 4))) / kcount
    centred = grouped - first[:, None, None, :, None] - normed_grouped * second[:, None, None, :, None]
    through = mask * (scale[:, None, None, :, None] * centred).reshape(normed.shape)
    grad_w = weight_slope(padded, slope)
    return (grads.astype(jnp.float32) + through, grad_w)

def reference(signals, conv_weight, buckets):
    samples = TOKENS // (SIDE * SIDE)
    pixels = jnp.roll(signals, TOK_DEV, axis=0)
    grid = pixels.reshape(samples, SIDE, SIDE, 2 * C)
    per_micro = samples // MICRO
    micro_of = (jnp.arange(samples) // per_micro).astype(jnp.int32)
    live_h = 16 + 2 * buckets[micro_of, 0]
    live_w = 16 + 2 * buckets[micro_of, 1]
    cells = jnp.arange(SIDE)
    inside = (cells[None, :, None] < live_h[:, None, None]) & (cells[None, None, :] < live_w[:, None, None])
    mask = inside.astype(jnp.float32)[..., None]
    count = (live_h * live_w).astype(jnp.float32)
    start = (grid[..., :C].astype(jnp.float32) * mask).astype(jnp.bfloat16)
    cotangent = grid[..., C:]
    w_down = conv_weight[:, :, :C]
    w_up = conv_weight[:, :, C:]
    hidden, cache_down = block_forward(start, w_down, mask, count)
    output, cache_up = block_forward(hidden, w_up, mask, count)
    up_grads, grad_up = block_backward(cotangent, cache_up, w_up, mask, count)
    returned = up_grads.astype(jnp.bfloat16)
    down_grads, grad_down = block_backward(returned, cache_down, w_down, mask, count)
    input_grad = (mask * down_grads).astype(jnp.bfloat16)
    results = jnp.concatenate([input_grad, output], axis=-1).reshape(TOKENS, 2 * C)
    results = jnp.roll(results, -TOK_DEV, axis=0)
    grad_weight = jnp.concatenate([grad_down, grad_up], axis=-1)
    return (results, grad_weight)
```

```python
import jax
import jax.numpy as jnp
from jax import lax
from jax.experimental import pallas as pl
from jax.experimental.pallas import tpu as pltpu
from jax.sharding import Mesh
from jax.sharding import PartitionSpec as P


AX = ("xh", "core", "z", "xl", "y")
SIZES = (2, 2, 8, 2, 4)
WEIGHT_GROUP = ("z", "xl")
GROUP_WIDTH = 24
OWN = 96
PIX = 1024
SIDE = 32
TAPS = 9
PAIR = 2 * OWN
QUAD = 4 * OWN
LANES = TAPS * PAIR
EPS = 1e-05
F32 = jnp.float32
BF16 = jnp.bfloat16


def flat(xh, core, z, xl, y):
    return (((xh * 2 + core) * 8 + z) * 2 + xl) * 4 + y


def every():
    for xh in range(2):
        for core in range(2):
            for z in range(8):
                for xl in range(2):
                    for y in range(4):
                        yield xh, core, z, xl, y


def pixel_pairs(turn):
    pairs = []
    for xh, core, z, xl, y in every():
        slot = ((z * 2 + xl) * 4 + y + 1) % 64
        sample, piece = slot // 4, slot % 4
        u = (piece + turn) % 4
        pairs.append(
            (flat(xh, core, z, xl, y), flat(xh, u % 2, sample // 2, sample % 2, 2 * core + u // 2))
        )
    return pairs


def weight_pairs(second):
    pairs = []
    for xh, core, z, xl, y in every():
        b = (y & 1) ^ second
        if xh == 0:
            target = (0, z % 2, 2 * (z // 2) + xl, y >> 1, 2 * core + b)
        else:
            target = (1, b, 4 * core + 2 * (z % 2) + xl, y >> 1, z // 2)
        pairs.append((flat(xh, core, z, xl, y), flat(*target)))
    return pairs


def back(pairs):
    return [(b, a) for a, b in pairs]


def swap(value, axis):
    return lax.ppermute(value, axis, [(0, 1), (1, 0)])


def turn_y(value, d):
    return lax.ppermute(value, "y", [(i, (i + d) % 4) for i in range(4)])


def pixels():
    p = lax.broadcasted_iota(jnp.int32, (1, PIX), 1)
    return p >> 5, p & 31


def live(prm):
    row, col = pixels()
    return ((row < prm[3]) & (col < prm[4])).astype(F32)


def offsets(tap):
    return tap // 3 - 1, tap % 3 - 1


def moved(field, dr, dc):
    off = dr * SIDE + dc
    if off == 0:
        return field
    row, col = pixels()
    ok = (row + dr >= 0) & (row + dr < SIDE) & (col + dc >= 0) & (col + dc < SIDE)
    return jnp.where(ok, pltpu.roll(field, (-off) % PIX, 1), 0.0)


def group_sum(field):
    return jnp.sum(field.reshape(OWN // GROUP_WIDTH, GROUP_WIDTH, PIX), axis=(1, 2), keepdims=True)


def spread(stat):
    return jnp.broadcast_to(stat, (OWN // GROUP_WIDTH, GROUP_WIDTH, PIX)).reshape(OWN, PIX)


def normed_of(values, mask, count):
    masked = values * mask
    mean = group_sum(masked) / count
    var = group_sum(masked * masked) / count - mean * mean
    scale = spread(lax.rsqrt(var + EPS))
    return (values - spread(mean)) * scale, scale


def count_of(prm):
    return (prm[3] * prm[4] * GROUP_WIDTH).astype(F32)


def silu_slope(u, s):
    return s * (1.0 + u * (1.0 - s))


def input_slope(e, xhat, scale, mask, count):
    m1 = spread(group_sum(e) / count)
    m2 = spread(group_sum(e * xhat) / count)
    return mask * (e - m1 - xhat * m2) * scale


def rows(k, n=OWN):
    return pl.ds(pl.multiple_of(k * n, n), n)


def split_kernel(prm, x_ref, *refs):
    outs, scratch = refs[:4], refs[4]
    scratch[...] = x_ref[...].astype(F32).T.astype(BF16)
    for v in range(4):
        outs[v][...] = scratch[rows((prm[5] + v) % 4), :]


def join_kernel(prm, *refs):
    ins, out, scratch = refs[:4], refs[4], refs[5]
    for v in range(4):
        scratch[rows((prm[5] + v) % 4), :] = ins[v][...]
    out[...] = scratch[...].astype(F32).T.astype(BF16)


def start_kernel(prm, *refs):
    ins, x_out, a_out = refs[:4], refs[4], refs[5]
    u = 2 * (prm[2] % 2) + prm[1]
    for v in range(4):
        t = (u - v + 4) % 4
        x_out[:, pl.ds(pl.multiple_of(t * 256, 256), 256)] = ins[v][...]
    mask = live(prm)
    values = x_out[...].astype(F32) * mask
    xhat, _ = normed_of(values, mask, count_of(prm))
    act = mask * (xhat * jax.nn.sigmoid(xhat))
    a_out[...] = jnp.where(prm[0] == 0, act, values).astype(BF16)


def convolve(w, act):
    acc = jnp.zeros((PAIR, PIX), F32)
    for tap in range(0, TAPS, 2):
        n = min(2, TAPS - tap)
        part = lax.dot_general(
            w[:, tap * PAIR : (tap + n) * PAIR],
            act,
            (((0,), (0,)), ((), ())),
            preferred_element_type=F32,
        )
        for k in range(n):
            acc = acc + moved(part[k * PAIR : (k + 1) * PAIR], *offsets(tap + k))
    return acc


def build_moved(act, d_ref):
    act = act.astype(F32)
    for tap in range(TAPS):
        dr, dc = offsets(tap)
        d_ref[tap * PAIR : (tap + 1) * PAIR, :] = moved(act, -dr, -dc).astype(BF16)


def gather_chunks(prm, own, others, full):
    full[rows(prm[2]), :] = own[...]
    for d, ref in enumerate(others, 1):
        full[rows((prm[2] + 4 - d) % 4), :] = ref[...]


def first_kernel(prm, w, a0, a1, a2, a3, full, keep, send, d_ref, res):
    gather_chunks(prm, a0, (a1, a2, a3), full)

    @pl.when(prm[0] == 0)
    def _():
        res[...] = convolve(w[...], full[...])

    @pl.when(prm[0] == 1)
    def _():
        for k in range(2):
            build_moved(full[k * PAIR : (k + 1) * PAIR, :], d_ref)
            part = jnp.dot(
                w[k * PAIR : (k + 1) * PAIR, :], d_ref[...], preferred_element_type=F32
            )
            if k == 0:
                res[...] = part
            else:
                res[...] += part

    keep[...] = res[rows(prm[1]), :]
    send[...] = res[rows(1 - prm[1]), :]


def middle_kernel(prm, x, keep, got, out):
    mask = live(prm)
    total = keep[...] + got[...]
    values = x[...].astype(F32) * mask
    out[...] = jnp.where(prm[0] == 0, values + mask * total, total).astype(BF16)


def turn_kernel(prm, mine, theirs, g, b_out, q_out):
    mask = live(prm)
    count = count_of(prm)
    down = prm[0] == 0
    hidden = jnp.where(down, mine[...].astype(F32), theirs[...].astype(F32))
    xhat, scale = normed_of(hidden, mask, count)
    s = jax.nn.sigmoid(xhat)

    @pl.when(down)
    def _():
        e = mask * theirs[...].astype(F32) * silu_slope(xhat, s)
        dv = (g[...].astype(F32) + input_slope(e, xhat, scale, mask, count)).astype(BF16)
        q_out[...] = dv
        b_out[...] = (dv.astype(F32) * mask).astype(BF16)

    @pl.when(jnp.logical_not(down))
    def _():
        q_out[...] = theirs[...]
        b_out[...] = (mask * (xhat * s)).astype(BF16)


def pair_up(prm, own, other, pair):
    pair[rows(prm[1]), :] = own[...]
    pair[rows(1 - prm[1]), :] = other[...]


def weight_slope_kernel(prm, full, b_own, b_other, dw, pair, d_ref):
    pair_up(prm, b_own, b_other, pair)

    def product(lhs):
        return lax.dot_general(
            lhs, d_ref[...], (((1,), (1,)), ((), ())), preferred_element_type=F32
        ).astype(BF16)

    @pl.when(prm[0] == 0)
    def _():
        build_moved(pair[...], d_ref)
        dw[...] = product(full[...])

    @pl.when(prm[0] == 1)
    def _():
        for k in range(2):
            build_moved(full[k * PAIR : (k + 1) * PAIR, :], d_ref)
            dw[k * PAIR : (k + 1) * PAIR, :] = product(pair[...])


def second_kernel(prm, w, b_own, b_other, keep, s1, s2, s3, pair, d_ref, res):
    pair_up(prm, b_own, b_other, pair)

    @pl.when(prm[0] == 0)
    def _():
        build_moved(pair[...], d_ref)
        res[...] = jnp.dot(w[...], d_ref[...], preferred_element_type=F32)

    @pl.when(prm[0] == 1)
    def _():
        for k in range(2):
            res[k * PAIR : (k + 1) * PAIR, :] = convolve(
                w[k * PAIR : (k + 1) * PAIR, :], pair[...]
            )

    keep[...] = res[rows(prm[2]), :]
    for d, ref in enumerate((s1, s2, s3), 1):
        ref[...] = res[rows((prm[2] + d) % 4), :].astype(BF16)


def last_kernel(prm, x, q, keep, r1, r2, r3, *refs):
    outs, scratch = refs[:4], refs[4]
    mask = live(prm)
    count = count_of(prm)
    total = keep[...] + r1[...].astype(F32) + r2[...].astype(F32) + r3[...].astype(F32)
    carried = q[...].astype(F32)

    @pl.when(prm[0] == 0)
    def _():
        xhat, scale = normed_of(x[...].astype(F32) * mask, mask, count)
        e = mask * total * silu_slope(xhat, jax.nn.sigmoid(xhat))
        slope = input_slope(e, xhat, scale, mask, count)
        scratch[...] = (mask * (carried + slope)).astype(BF16)

    @pl.when(prm[0] == 1)
    def _():
        scratch[...] = (carried + mask * total).astype(BF16)

    u = 2 * (prm[2] % 2) + prm[1]
    for v in range(4):
        t = (u - v + 4) % 4
        outs[v][...] = scratch[:, pl.ds(pl.multiple_of(t * 256, 256), 256)]


def call(kernel, outs, scratch, prm, *args):
    vmem = pl.BlockSpec(memory_space=pltpu.VMEM)
    return pl.pallas_call(
        kernel,
        out_shape=[jax.ShapeDtypeStruct(s, d) for s, d in outs],
        in_specs=[pl.BlockSpec(memory_space=pltpu.SMEM)] + [vmem] * len(args),
        out_specs=[vmem] * len(outs),
        scratch_shapes=[pltpu.VMEM(s, d) for s, d in scratch],
    )(prm, *args)


def per_device(signals, conv_weight, buckets):
    xh, core, z, xl, y = (lax.axis_index(a) for a in AX)
    micro = z // 4
    own_bucket = jnp.where(micro == 0, buckets[0], buckets[1])
    size = 16 + 2 * own_bucket
    piece = (y + 1) % 4
    prm = jnp.stack([xh, core, y, size[0], size[1], piece]).astype(jnp.int32)
    own = ((OWN, PIX), BF16)
    own32 = ((OWN, PIX), F32)

    cut = conv_weight.reshape(12, TAPS, 4, OWN)
    low = jnp.where(xh == 0, cut[:, :, 0:2], cut[:, :, 0::2]).reshape(12, LANES)
    high = jnp.where(xh == 0, cut[:, :, 2:4], cut[:, :, 1::2]).reshape(12, LANES)
    odd = y % 2 == 1
    got = [
        lax.ppermute(jnp.where(odd, high, low), AX, weight_pairs(0)),
        lax.ppermute(jnp.where(odd, low, high), AX, weight_pairs(1)),
    ]
    flip = jnp.where(xh == 0, y % 2, core) == 1
    part = jnp.concatenate([jnp.where(flip, got[1], got[0]), jnp.where(flip, got[0], got[1])], 0)
    copies = jnp.broadcast_to(part, (16, 24, LANES))
    w = lax.all_to_all(copies, WEIGHT_GROUP, 0, 0, tiled=True).reshape(QUAD, LANES)

    blocks = call(
        split_kernel, [((OWN, 256), BF16)] * 4, [((QUAD, 256), BF16)], prm, signals
    )
    blocks = [lax.ppermute(b, AX, pixel_pairs(v)) for v, b in enumerate(blocks)]
    x, a = call(start_kernel, [own, own], [], prm, *blocks)
    g = swap(x, "xh")
    others = [turn_y(a, d) for d in (1, 2, 3)]

    full, keep, send = call(
        first_kernel,
        [((QUAD, PIX), BF16), own32, own32],
        [((LANES, PIX), BF16), ((PAIR, PIX), F32)],
        prm,
        w,
        a,
        *others,
    )
    (mine,) = call(middle_kernel, [own], [], prm, x, keep, swap(send, "core"))
    theirs = swap(mine, "xh")
    b, q = call(turn_kernel, [own, own], [], prm, mine, theirs, g)
    b_other = swap(b, "core")
    (dw,) = call(
        weight_slope_kernel,
        [((QUAD, LANES), BF16)],
        [((PAIR, PIX), BF16), ((LANES, PIX), BF16)],
        prm,
        full,
        b,
        b_other,
    )
    keep, *sends = call(
        second_kernel,
        [own32, own, own, own],
        [((PAIR, PIX), BF16), ((LANES, PIX), BF16), ((QUAD, PIX), F32)],
        prm,
        w,
        b,
        b_other,
    )
    got = [turn_y(s, d) for d, s in enumerate(sends, 1)]
    blocks = call(last_kernel, [((OWN, 256), BF16)] * 4, [own], prm, x, q, keep, *got)
    blocks = [lax.ppermute(b, AX, back(pixel_pairs(v))) for v, b in enumerate(blocks)]
    (results,) = call(
        join_kernel, [((256, QUAD), BF16)], [((QUAD, 256), BF16)], prm, *blocks
    )

    shares = lax.all_to_all(dw.reshape(16, 24, LANES), WEIGHT_GROUP, 0, 0, tiled=True)
    total = jnp.sum(shares.astype(F32), axis=0)
    first, second = total[:12], total[12:]
    low_high = [
        lax.ppermute(jnp.where(flip, second, first), AX, back(weight_pairs(0))),
        lax.ppermute(jnp.where(flip, first, second), AX, back(weight_pairs(1))),
    ]
    low = jnp.where(odd, low_high[1], low_high[0]).reshape(12, TAPS, 2, OWN)
    high = jnp.where(odd, low_high[0], low_high[1]).reshape(12, TAPS, 2, OWN)
    apart = jnp.concatenate([low, high], axis=2)
    woven = jnp.stack([low, high], axis=3).reshape(12, TAPS, 4, OWN)
    grad_weight = jnp.where(xh == 0, apart, woven).reshape(12, TAPS, QUAD)
    return results, grad_weight


def solution(mesh):
    finer = Mesh(mesh.devices.reshape(SIZES), AX)
    section, fsdp = ("xh", "core"), ("z", "xl", "y")
    placed = (P(fsdp, section), P(fsdp, None, section), P())
    return jax.shard_map(
        per_device,
        mesh=finer,
        in_specs=placed,
        out_specs=(P(fsdp, section), P(fsdp, None, section)),
        check_vma=False,
    )
```

```python
import jax
import jax.numpy as jnp
from jax import lax
from jax.experimental import pallas as pl
from jax.experimental.pallas import tpu as pltpu
from jax.sharding import Mesh
from jax.sharding import PartitionSpec as P


AX = ("xh", "core", "z", "xl", "y")
SIZES = (2, 2, 8, 2, 4)
WEIGHT_GROUP = ("z", "xl")
GROUP_WIDTH = 24
OWN = 96
PIX = 1024
SIDE = 32
TAPS = 9
PAIR = 2 * OWN
QUAD = 4 * OWN
LANES = TAPS * PAIR
EPS = 1e-05
F32 = jnp.float32
BF16 = jnp.bfloat16


def flat(xh, core, z, xl, y):
    return (((xh * 2 + core) * 8 + z) * 2 + xl) * 4 + y


def every():
    for xh in range(2):
        for core in range(2):
            for z in range(8):
                for xl in range(2):
                    for y in range(4):
                        yield xh, core, z, xl, y


def pixel_pairs(turn):
    pairs = []
    for xh, core, z, xl, y in every():
        slot = ((z * 2 + xl) * 4 + y + 1) % 64
        sample, piece = slot // 4, slot % 4
        u = (piece + turn) % 4
        pairs.append(
            (flat(xh, core, z, xl, y), flat(xh, u % 2, sample // 2, sample % 2, 2 * core + u // 2))
        )
    return pairs


def weight_pairs(second):
    pairs = []
    for xh, core, z, xl, y in every():
        b = (y & 1) ^ second
        if xh == 0:
            target = (0, z % 2, 2 * (z // 2) + xl, y >> 1, 2 * core + b)
        else:
            target = (1, b, 4 * core + 2 * (z % 2) + xl, y >> 1, z // 2)
        pairs.append((flat(xh, core, z, xl, y), flat(*target)))
    return pairs


def back(pairs):
    return [(b, a) for a, b in pairs]


def swap(value, axis):
    return lax.ppermute(value, axis, [(0, 1), (1, 0)])


def turn_y(value, d):
    return lax.ppermute(value, "y", [(i, (i + d) % 4) for i in range(4)])


def pixels():
    p = lax.broadcasted_iota(jnp.int32, (1, PIX), 1)
    return p >> 5, p & 31


def live(prm):
    row, col = pixels()
    return ((row < prm[3]) & (col < prm[4])).astype(F32)


def offsets(tap):
    return tap // 3 - 1, tap % 3 - 1


def moved(field, dr, dc):
    off = dr * SIDE + dc
    if off == 0:
        return field
    row, col = pixels()
    ok = (row + dr >= 0) & (row + dr < SIDE) & (col + dc >= 0) & (col + dc < SIDE)
    return jnp.where(ok, pltpu.roll(field, (-off) % PIX, 1), 0.0)


def group_sum(field):
    return jnp.sum(field.reshape(OWN // GROUP_WIDTH, GROUP_WIDTH, PIX), axis=(1, 2), keepdims=True)


def spread(stat):
    return jnp.broadcast_to(stat, (OWN // GROUP_WIDTH, GROUP_WIDTH, PIX)).reshape(OWN, PIX)


def normed_of(values, mask, count):
    masked = values * mask
    mean = group_sum(masked) / count
    var = group_sum(masked * masked) / count - mean * mean
    scale = spread(lax.rsqrt(var + EPS))
    return (values - spread(mean)) * scale, scale


def count_of(prm):
    return (prm[3] * prm[4] * GROUP_WIDTH).astype(F32)


def silu_slope(u, s):
    return s * (1.0 + u * (1.0 - s))


def input_slope(e, xhat, scale, mask, count):
    m1 = spread(group_sum(e) / count)
    m2 = spread(group_sum(e * xhat) / count)
    return mask * (e - m1 - xhat * m2) * scale


def rows(k, n=OWN):
    return pl.ds(pl.multiple_of(k * n, n), n)


def split_kernel(prm, x_ref, *refs):
    outs, scratch = refs[:4], refs[4]
    scratch[...] = x_ref[...].astype(F32).T.astype(BF16)
    for v in range(4):
        outs[v][...] = scratch[rows((prm[5] + v) % 4), :]


def join_kernel(prm, *refs):
    ins, out, scratch = refs[:4], refs[4], refs[5]
    for v in range(4):
        scratch[rows((prm[5] + v) % 4), :] = ins[v][...]
    out[...] = scratch[...].astype(F32).T.astype(BF16)


def start_kernel(prm, *refs):
    ins, x_out, a_out = refs[:4], refs[4], refs[5]
    u = 2 * (prm[2] % 2) + prm[1]
    for v in range(4):
        t = (u - v + 4) % 4
        x_out[:, pl.ds(pl.multiple_of(t * 256, 256), 256)] = ins[v][...]
    mask = live(prm)
    values = x_out[...].astype(F32) * mask
    xhat, _ = normed_of(values, mask, count_of(prm))
    act = mask * (xhat * jax.nn.sigmoid(xhat))
    a_out[...] = jnp.where(prm[0] == 0, act, values).astype(BF16)


def convolve(w, act):
    acc = jnp.zeros((PAIR, PIX), F32)
    for tap in range(0, TAPS, 2):
        n = min(2, TAPS - tap)
        part = lax.dot_general(
            w[:, tap * PAIR : (tap + n) * PAIR],
            act,
            (((0,), (0,)), ((), ())),
            preferred_element_type=F32,
        )
        for k in range(n):
            acc = acc + moved(part[k * PAIR : (k + 1) * PAIR], *offsets(tap + k))
    return acc


def build_moved(act, d_ref):
    act = act.astype(F32)
    for tap in range(TAPS):
        dr, dc = offsets(tap)
        d_ref[tap * PAIR : (tap + 1) * PAIR, :] = moved(act, -dr, -dc).astype(BF16)


def gather_chunks(prm, own, others, full):
    full[rows(prm[2]), :] = own[...]
    for d, ref in enumerate(others, 1):
        full[rows((prm[2] + 4 - d) % 4), :] = ref[...]


def first_kernel(prm, w, g, a0, a1, a2, a3, full, keep, send, d_ref, res):
    gather_chunks(prm, a0, (a1, a2, a3), full)

    @pl.when(prm[0] == 0)
    def _():
        res[...] = convolve(w[...], full[...])

    @pl.when(prm[0] == 1)
    def _():
        for k in range(2):
            build_moved(full[k * PAIR : (k + 1) * PAIR, :], d_ref)
            part = jnp.dot(
                w[k * PAIR : (k + 1) * PAIR, :], d_ref[...], preferred_element_type=F32
            )
            if k == 0:
                res[...] = part
            else:
                res[...] += part

    keep[...] = res[rows(prm[1]), :]
    send[...] = res[rows(1 - prm[1]), :]


def middle_kernel(prm, x, keep, got, out):
    mask = live(prm)
    total = keep[...] + got[...]
    values = x[...].astype(F32) * mask
    out[...] = jnp.where(prm[0] == 0, values + mask * total, total).astype(BF16)


def turn_kernel(prm, mine, theirs, g, b_out, q_out):
    mask = live(prm)
    count = count_of(prm)
    down = prm[0] == 0
    hidden = jnp.where(down, mine[...].astype(F32), theirs[...].astype(F32))
    xhat, scale = normed_of(hidden, mask, count)
    s = jax.nn.sigmoid(xhat)

    @pl.when(down)
    def _():
        e = mask * theirs[...].astype(F32) * silu_slope(xhat, s)
        dv = (g[...].astype(F32) + input_slope(e, xhat, scale, mask, count)).astype(BF16)
        q_out[...] = dv
        b_out[...] = (dv.astype(F32) * mask).astype(BF16)

    @pl.when(jnp.logical_not(down))
    def _():
        q_out[...] = theirs[...]
        b_out[...] = (mask * (xhat * s)).astype(BF16)


def pair_up(prm, own, other, pair):
    pair[rows(prm[1]), :] = own[...]
    pair[rows(1 - prm[1]), :] = other[...]


def weight_slope_kernel(prm, full, b_own, b_other, dw, pair, d_ref):
    pair_up(prm, b_own, b_other, pair)

    def product(lhs):
        return lax.dot_general(
            lhs, d_ref[...], (((1,), (1,)), ((), ())), preferred_element_type=F32
        ).astype(BF16)

    @pl.when(prm[0] == 0)
    def _():
        build_moved(pair[...], d_ref)
        dw[...] = product(full[...])

    @pl.when(prm[0] == 1)
    def _():
        for k in range(2):
            build_moved(full[k * PAIR : (k + 1) * PAIR, :], d_ref)
            dw[k * PAIR : (k + 1) * PAIR, :] = product(pair[...])


def second_kernel(prm, w, b_own, b_other, keep, s1, s2, s3, pair, d_ref, res):
    pair_up(prm, b_own, b_other, pair)

    @pl.when(prm[0] == 0)
    def _():
        build_moved(pair[...], d_ref)
        res[...] = jnp.dot(w[...], d_ref[...], preferred_element_type=F32)

    @pl.when(prm[0] == 1)
    def _():
        for k in range(2):
            res[k * PAIR : (k + 1) * PAIR, :] = convolve(
                w[k * PAIR : (k + 1) * PAIR, :], pair[...]
            )

    keep[...] = res[rows(prm[2]), :]
    for d, ref in enumerate((s1, s2, s3), 1):
        ref[...] = res[rows((prm[2] + d) % 4), :].astype(BF16)


def last_kernel(prm, x, q, keep, r1, r2, r3, *refs):
    outs, scratch = refs[:4], refs[4]
    mask = live(prm)
    count = count_of(prm)
    total = keep[...] + r1[...].astype(F32) + r2[...].astype(F32) + r3[...].astype(F32)
    carried = q[...].astype(F32)

    @pl.when(prm[0] == 0)
    def _():
        xhat, scale = normed_of(x[...].astype(F32) * mask, mask, count)
        e = mask * total * silu_slope(xhat, jax.nn.sigmoid(xhat))
        slope = input_slope(e, xhat, scale, mask, count)
        scratch[...] = (mask * (carried + slope)).astype(BF16)

    @pl.when(prm[0] == 1)
    def _():
        scratch[...] = (carried + mask * total).astype(BF16)

    u = 2 * (prm[2] % 2) + prm[1]
    for v in range(4):
        t = (u - v + 4) % 4
        outs[v][...] = scratch[:, pl.ds(pl.multiple_of(t * 256, 256), 256)]


def call(kernel, outs, scratch, prm, *args, grant=8):
    vmem = pl.BlockSpec(memory_space=pltpu.VMEM)
    return pl.pallas_call(
        kernel,
        out_shape=[jax.ShapeDtypeStruct(s, d) for s, d in outs],
        in_specs=[pl.BlockSpec(memory_space=pltpu.SMEM)] + [vmem] * len(args),
        out_specs=[vmem] * len(outs),
        scratch_shapes=[pltpu.VMEM(s, d) for s, d in scratch],
        compiler_params=pltpu.CompilerParams(vmem_limit_bytes=grant << 20),
    )(prm, *args)


def step(signals, conv_weight, buckets):
    xh, core, z, _, y = (lax.axis_index(a) for a in AX)
    micro = z // 4
    own_bucket = jnp.where(micro == 0, buckets[0], buckets[1])
    size = 16 + 2 * own_bucket
    piece = (y + 1) % 4
    prm = jnp.stack([xh, core, y, size[0], size[1], piece]).astype(jnp.int32)
    own = ((OWN, PIX), BF16)
    own32 = ((OWN, PIX), F32)

    cut = conv_weight.reshape(12, TAPS, 4, OWN)
    low = jnp.where(xh == 0, cut[:, :, 0:2], cut[:, :, 0::2]).reshape(12, LANES)
    high = jnp.where(xh == 0, cut[:, :, 2:4], cut[:, :, 1::2]).reshape(12, LANES)
    odd = y % 2 == 1
    got = [
        lax.ppermute(jnp.where(odd, high, low), AX, weight_pairs(0)),
        lax.ppermute(jnp.where(odd, low, high), AX, weight_pairs(1)),
    ]
    flip = jnp.where(xh == 0, y % 2, core) == 1
    part = jnp.concatenate([jnp.where(flip, got[1], got[0]), jnp.where(flip, got[0], got[1])], 0)
    copies = jnp.broadcast_to(part, (16, 24, LANES))
    w = lax.all_to_all(copies, WEIGHT_GROUP, 0, 0, tiled=True).reshape(QUAD, LANES)

    blocks = call(
        split_kernel, [((OWN, 256), BF16)] * 4, [((QUAD, 256), BF16)], prm, signals
    )
    blocks = [lax.ppermute(b, AX, pixel_pairs(v)) for v, b in enumerate(blocks)]
    x, a = call(start_kernel, [own, own], [], prm, *blocks)
    others = [turn_y(a, d) for d in (1, 2, 3)]
    g = swap(x, "xh")

    full, keep, send = call(
        first_kernel,
        [((QUAD, PIX), BF16), own32, own32],
        [((LANES, PIX), BF16), ((PAIR, PIX), F32)],
        prm,
        w,
        g,
        a,
        *others,
        grant=24,
    )
    (mine,) = call(middle_kernel, [own], [], prm, x, keep, swap(send, "core"))
    theirs = swap(mine, "xh")
    b, q = call(turn_kernel, [own, own], [], prm, mine, theirs, g)
    b_other = swap(b, "core")
    (dw,) = call(
        weight_slope_kernel,
        [((QUAD, LANES), BF16)],
        [((PAIR, PIX), BF16), ((LANES, PIX), BF16)],
        prm,
        full,
        b,
        b_other,
        grant=24,
    )
    keep, *sends = call(
        second_kernel,
        [own32, own, own, own],
        [((PAIR, PIX), BF16), ((LANES, PIX), BF16), ((QUAD, PIX), F32)],
        prm,
        w,
        b,
        b_other,
        grant=24,
    )
    got = [turn_y(s, d) for d, s in enumerate(sends, 1)]
    blocks = call(last_kernel, [((OWN, 256), BF16)] * 4, [own], prm, x, q, keep, *got)
    blocks = [lax.ppermute(b, AX, back(pixel_pairs(v))) for v, b in enumerate(blocks)]
    (results,) = call(
        join_kernel, [((256, QUAD), BF16)], [((QUAD, 256), BF16)], prm, *blocks
    )

    shares = lax.all_to_all(dw.reshape(16, 24, LANES), WEIGHT_GROUP, 0, 0, tiled=True)
    total = jnp.sum(shares.astype(F32), axis=0)
    first, second = total[:12], total[12:]
    low_high = [
        lax.ppermute(jnp.where(flip, second, first), AX, back(weight_pairs(0))),
        lax.ppermute(jnp.where(flip, first, second), AX, back(weight_pairs(1))),
    ]
    low = jnp.where(odd, low_high[1], low_high[0]).reshape(12, TAPS, 2, OWN)
    high = jnp.where(odd, low_high[0], low_high[1]).reshape(12, TAPS, 2, OWN)
    apart = jnp.concatenate([low, high], axis=2)
    woven = jnp.stack([low, high], axis=3).reshape(12, TAPS, 4, OWN)
    grad_weight = jnp.where(xh == 0, apart, woven).reshape(12, TAPS, QUAD)
    return results, grad_weight


def solution(mesh):
    finer = Mesh(mesh.devices.reshape(SIZES), AX)
    section, fsdp = ("xh", "core"), ("z", "xl", "y")
    placed = (P(fsdp, section), P(fsdp, None, section), P())
    return jax.shard_map(
        step,
        mesh=finer,
        in_specs=placed,
        out_specs=(P(fsdp, section), P(fsdp, None, section)),
        check_vma=False,
    )
```

```python
import jax
import jax.numpy as jnp
from jax import lax
from jax.experimental import pallas as pl
from jax.experimental.pallas import tpu as pltpu
from jax.sharding import Mesh
from jax.sharding import PartitionSpec as P


AX = ("xh", "core", "z", "xl", "y")
SIZES = (2, 2, 8, 2, 4)
WEIGHT_GROUP = ("z", "xl")
FSDP = ("z", "xl", "y")
GROUP_WIDTH = 24
OWN = 96
PIX = 1024
SIDE = 32
TAPS = 9
PAIR = 2 * OWN
QUAD = 4 * OWN
LANES = TAPS * PAIR
EPS = 1e-05
F32 = jnp.float32
BF16 = jnp.bfloat16


def flat(xh, core, z, xl, y):
    return (((xh * 2 + core) * 8 + z) * 2 + xl) * 4 + y


def every():
    for xh in range(2):
        for core in range(2):
            for z in range(8):
                for xl in range(2):
                    for y in range(4):
                        yield xh, core, z, xl, y


def pixel_pairs(turn, ahead):
    pairs = []
    for xh, core, z, xl, y in every():
        slot = ((z * 2 + xl) * 4 + y + ahead) % 64
        sample, piece = slot // 4, slot % 4
        u = (piece + turn) % 4
        pairs.append(
            (flat(xh, core, z, xl, y), flat(xh, u % 2, sample // 2, sample % 2, 2 * core + u // 2))
        )
    return pairs


def weight_pairs(second):
    pairs = []
    for xh, core, z, xl, y in every():
        b = (y & 1) ^ second
        if xh == 0:
            target = (0, z % 2, 2 * (z // 2) + xl, y >> 1, 2 * core + b)
        else:
            target = (1, b, 4 * core + 2 * (z % 2) + xl, y >> 1, z // 2)
        pairs.append((flat(xh, core, z, xl, y), flat(*target)))
    return pairs


def back(pairs):
    return [(b, a) for a, b in pairs]


def swap(value, axis):
    return lax.ppermute(value, axis, [(0, 1), (1, 0)])


def turn_y(value, d):
    return lax.ppermute(value, "y", [(i, (i + d) % 4) for i in range(4)])


def pixels():
    p = lax.broadcasted_iota(jnp.int32, (1, PIX), 1)
    return p >> 5, p & 31


def live(prm):
    row, col = pixels()
    return ((row < prm[3]) & (col < prm[4])).astype(F32)


def offsets(tap):
    return tap // 3 - 1, tap % 3 - 1


def moved(field, dr, dc):
    off = dr * SIDE + dc
    if off == 0:
        return field
    row, col = pixels()
    ok = (row + dr >= 0) & (row + dr < SIDE) & (col + dc >= 0) & (col + dc < SIDE)
    return pltpu.roll(field, (-off) % PIX, 1) * ok.astype(F32).astype(field.dtype)


def group_sum(field):
    return jnp.sum(field.reshape(OWN // GROUP_WIDTH, GROUP_WIDTH, PIX), axis=(1, 2), keepdims=True)


def spread(stat):
    return jnp.broadcast_to(stat, (OWN // GROUP_WIDTH, GROUP_WIDTH, PIX)).reshape(OWN, PIX)


def normed_of(values, mask, count):
    masked = values * mask
    mean = group_sum(masked) / count
    var = group_sum(masked * masked) / count - mean * mean
    scale = spread(lax.rsqrt(var + EPS))
    return (values - spread(mean)) * scale, scale


def count_of(prm):
    return (prm[3] * prm[4] * GROUP_WIDTH).astype(F32)


def silu_slope(u, s):
    return s * (1.0 + u * (1.0 - s))


def input_slope(e, xhat, scale, mask, count):
    m1 = spread(group_sum(e) / count)
    m2 = spread(group_sum(e * xhat) / count)
    return mask * (e - m1 - xhat * m2) * scale


def rows(k, n=OWN):
    return pl.ds(pl.multiple_of(k * n, n), n)


def split_kernel(prm, x_ref, *refs):
    outs, scratch = refs[:4], refs[4]
    scratch[...] = x_ref[...].astype(F32).T.astype(BF16)
    for v in range(4):
        outs[v][...] = scratch[rows((prm[2] + v) % 4), :]


def join_kernel(prm, *refs):
    ins, out, scratch = refs[:4], refs[4], refs[5]
    for v in range(4):
        scratch[rows((prm[5] + v) % 4), :] = ins[v][...]
    out[...] = scratch[...].astype(F32).T.astype(BF16)


def start_kernel(prm, *refs):
    ins, x_out, a_out = refs[:4], refs[4], refs[5]
    u = 2 * (prm[2] % 2) + prm[1]
    for v in range(4):
        t = (u - v + 4) % 4
        x_out[:, pl.ds(pl.multiple_of(t * 256, 256), 256)] = ins[v][...]
    mask = live(prm)
    values = x_out[...].astype(F32) * mask
    xhat, _ = normed_of(values, mask, count_of(prm))
    act = mask * (xhat * jax.nn.sigmoid(xhat))
    a_out[...] = jnp.where(prm[0] == 0, act, values).astype(BF16)


def convolve(w, act):
    acc = jnp.zeros((PAIR, PIX), F32)
    for tap in range(0, TAPS, 2):
        n = min(2, TAPS - tap)
        part = lax.dot_general(
            w[:, tap * PAIR : (tap + n) * PAIR],
            act,
            (((0,), (0,)), ((), ())),
            preferred_element_type=F32,
        )
        for k in range(n):
            acc = acc + moved(part[k * PAIR : (k + 1) * PAIR], *offsets(tap + k))
    return acc


def build_moved(act, d_ref):
    for tap in range(TAPS):
        dr, dc = offsets(tap)
        d_ref[tap * PAIR : (tap + 1) * PAIR, :] = moved(act, -dr, -dc)


def gather_chunks(prm, own, others, full):
    full[rows(prm[2]), :] = own[...]
    for d, ref in enumerate(others, 1):
        full[rows((prm[2] + 4 - d) % 4), :] = ref[...]


def first_kernel(prm, w, g, a0, a1, a2, a3, full, keep, send, d_ref, res):
    gather_chunks(prm, a0, (a1, a2, a3), full)

    @pl.when(prm[0] == 0)
    def _():
        res[...] = convolve(w[...], full[...])

    @pl.when(prm[0] == 1)
    def _():
        for k in range(2):
            build_moved(full[k * PAIR : (k + 1) * PAIR, :], d_ref)
            part = jnp.dot(
                w[k * PAIR : (k + 1) * PAIR, :], d_ref[...], preferred_element_type=F32
            )
            if k == 0:
                res[...] = part
            else:
                res[...] += part

    keep[...] = res[rows(prm[1]), :]
    send[...] = res[rows(1 - prm[1]), :]


def middle_kernel(prm, x, keep, got, out):
    mask = live(prm)
    total = keep[...] + got[...]
    values = x[...].astype(F32) * mask
    out[...] = jnp.where(prm[0] == 0, values + mask * total, total).astype(BF16)


def turn_kernel(prm, mine, theirs, g, b_out, q_out):
    mask = live(prm)
    count = count_of(prm)
    down = prm[0] == 0
    hidden = jnp.where(down, mine[...].astype(F32), theirs[...].astype(F32))
    xhat, scale = normed_of(hidden, mask, count)
    s = jax.nn.sigmoid(xhat)

    @pl.when(down)
    def _():
        e = mask * theirs[...].astype(F32) * silu_slope(xhat, s)
        dv = (g[...].astype(F32) + input_slope(e, xhat, scale, mask, count)).astype(BF16)
        q_out[...] = dv
        b_out[...] = (dv.astype(F32) * mask).astype(BF16)

    @pl.when(jnp.logical_not(down))
    def _():
        q_out[...] = theirs[...]
        b_out[...] = (mask * (xhat * s)).astype(BF16)


def pair_up(prm, own, other, pair):
    pair[rows(prm[1]), :] = own[...]
    pair[rows(1 - prm[1]), :] = other[...]


def weight_slope_kernel(prm, full, b_own, b_other, dw, pair, d_ref):
    pair_up(prm, b_own, b_other, pair)

    def product(lhs):
        return lax.dot_general(
            lhs, d_ref[...], (((1,), (1,)), ((), ())), preferred_element_type=F32
        ).astype(BF16)

    @pl.when(prm[0] == 0)
    def _():
        build_moved(pair[...], d_ref)
        dw[...] = product(full[...])

    @pl.when(prm[0] == 1)
    def _():
        for k in range(2):
            build_moved(full[k * PAIR : (k + 1) * PAIR, :], d_ref)
            dw[k * PAIR : (k + 1) * PAIR, :] = product(pair[...])


def second_kernel(prm, w, b_own, b_other, keep, s1, s2, s3, pair, d_ref, res):
    pair_up(prm, b_own, b_other, pair)

    @pl.when(prm[0] == 0)
    def _():
        build_moved(pair[...], d_ref)
        res[...] = jnp.dot(w[...], d_ref[...], preferred_element_type=F32)

    @pl.when(prm[0] == 1)
    def _():
        for k in range(2):
            res[k * PAIR : (k + 1) * PAIR, :] = convolve(
                w[k * PAIR : (k + 1) * PAIR, :], pair[...]
            )

    keep[...] = res[rows(prm[2]), :]
    for d, ref in enumerate((s1, s2, s3), 1):
        ref[...] = res[rows((prm[2] + d) % 4), :].astype(BF16)


def last_kernel(prm, x, q, keep, r1, r2, r3, *refs):
    outs, scratch = refs[:4], refs[4]
    mask = live(prm)
    count = count_of(prm)
    total = keep[...] + r1[...].astype(F32) + r2[...].astype(F32) + r3[...].astype(F32)
    carried = q[...].astype(F32)

    @pl.when(prm[0] == 0)
    def _():
        xhat, scale = normed_of(x[...].astype(F32) * mask, mask, count)
        e = mask * total * silu_slope(xhat, jax.nn.sigmoid(xhat))
        slope = input_slope(e, xhat, scale, mask, count)
        scratch[...] = (mask * (carried + slope)).astype(BF16)

    @pl.when(prm[0] == 1)
    def _():
        scratch[...] = (carried + mask * total).astype(BF16)

    u = 2 * (prm[2] % 2) + prm[1]
    for v in range(4):
        t = (u - v + 4) % 4
        outs[v][...] = scratch[:, pl.ds(pl.multiple_of(t * 256, 256), 256)]


def call(kernel, outs, scratch, prm, *args, grant=8):
    vmem = pl.BlockSpec(memory_space=pltpu.VMEM)
    return pl.pallas_call(
        kernel,
        out_shape=[jax.ShapeDtypeStruct(s, d) for s, d in outs],
        in_specs=[pl.BlockSpec(memory_space=pltpu.SMEM)] + [vmem] * len(args),
        out_specs=[vmem] * len(outs),
        scratch_shapes=[pltpu.VMEM(s, d) for s, d in scratch],
        compiler_params=pltpu.CompilerParams(vmem_limit_bytes=grant << 20),
    )(prm, *args)


def step(signals, conv_weight, buckets):
    xh, core, z, _, y = (lax.axis_index(a) for a in AX)
    micro = z // 4
    own_bucket = jnp.where(micro == 0, buckets[0], buckets[1])
    size = 16 + 2 * own_bucket
    piece = (y + 1) % 4
    prm = jnp.stack([xh, core, y, size[0], size[1], piece]).astype(jnp.int32)
    own = ((OWN, PIX), BF16)
    own32 = ((OWN, PIX), F32)

    cut = conv_weight.reshape(12, TAPS, 4, OWN)
    low = jnp.where(xh == 0, cut[:, :, 0:2], cut[:, :, 0::2]).reshape(12, LANES)
    high = jnp.where(xh == 0, cut[:, :, 2:4], cut[:, :, 1::2]).reshape(12, LANES)
    odd = y % 2 == 1
    got = [
        lax.ppermute(jnp.where(odd, high, low), AX, weight_pairs(0)),
        lax.ppermute(jnp.where(odd, low, high), AX, weight_pairs(1)),
    ]
    flip = jnp.where(xh == 0, y % 2, core) == 1
    part = jnp.concatenate([jnp.where(flip, got[1], got[0]), jnp.where(flip, got[0], got[1])], 0)
    copies = jnp.broadcast_to(part, (16, 24, LANES))
    w = lax.all_to_all(copies, WEIGHT_GROUP, 0, 0, tiled=True).reshape(QUAD, LANES)

    shifted = lax.ppermute(signals, FSDP, [(i, (i + 1) % 64) for i in range(64)])
    blocks = call(
        split_kernel, [((OWN, 256), BF16)] * 4, [((QUAD, 256), BF16)], prm, shifted
    )
    blocks = [lax.ppermute(b, AX, pixel_pairs(v, 0)) for v, b in enumerate(blocks)]
    x, a = call(start_kernel, [own, own], [], prm, *blocks)
    others = [turn_y(a, d) for d in (1, 2, 3)]
    g = swap(x, "xh")

    full, keep, send = call(
        first_kernel,
        [((QUAD, PIX), BF16), own32, own32],
        [((LANES, PIX), BF16), ((PAIR, PIX), F32)],
        prm,
        w,
        g,
        a,
        *others,
        grant=24,
    )
    (mine,) = call(middle_kernel, [own], [], prm, x, keep, swap(send, "core"))
    theirs = swap(mine, "xh")
    b, q = call(turn_kernel, [own, own], [], prm, mine, theirs, g)
    b_other = swap(b, "core")
    (dw,) = call(
        weight_slope_kernel,
        [((QUAD, LANES), BF16)],
        [((PAIR, PIX), BF16), ((LANES, PIX), BF16)],
        prm,
        full,
        b,
        b_other,
        grant=24,
    )
    keep, *sends = call(
        second_kernel,
        [own32, own, own, own],
        [((PAIR, PIX), BF16), ((LANES, PIX), BF16), ((QUAD, PIX), F32)],
        prm,
        w,
        b,
        b_other,
        grant=24,
    )
    got = [turn_y(s, d) for d, s in enumerate(sends, 1)]
    blocks = call(last_kernel, [((OWN, 256), BF16)] * 4, [own], prm, x, q, keep, *got)
    blocks = [lax.ppermute(b, AX, back(pixel_pairs(v, 1))) for v, b in enumerate(blocks)]
    (results,) = call(
        join_kernel, [((256, QUAD), BF16)], [((QUAD, 256), BF16)], prm, *blocks
    )

    shares = lax.all_to_all(dw.reshape(16, 24, LANES), WEIGHT_GROUP, 0, 0, tiled=True)
    total = jnp.sum(shares.astype(F32), axis=0).astype(BF16)
    first, second = total[:12], total[12:]
    low_high = [
        lax.ppermute(jnp.where(flip, second, first), AX, back(weight_pairs(0))),
        lax.ppermute(jnp.where(flip, first, second), AX, back(weight_pairs(1))),
    ]
    low = jnp.where(odd, low_high[1], low_high[0]).reshape(12, TAPS, 2, OWN)
    high = jnp.where(odd, low_high[0], low_high[1]).reshape(12, TAPS, 2, OWN)
    apart = jnp.concatenate([low, high], axis=2)
    woven = jnp.stack([low, high], axis=3).reshape(12, TAPS, 4, OWN)
    grad_weight = jnp.where(xh == 0, apart, woven).reshape(12, TAPS, QUAD).astype(F32)
    return results, grad_weight


def solution(mesh):
    finer = Mesh(mesh.devices.reshape(SIZES), AX)
    section, fsdp = ("xh", "core"), ("z", "xl", "y")
    placed = (P(fsdp, section), P(fsdp, None, section), P())
    return jax.shard_map(
        step,
        mesh=finer,
        in_specs=placed,
        out_specs=(P(fsdp, section), P(fsdp, None, section)),
        check_vma=False,
    )
```

```python
import jax
import jax.numpy as jnp
from jax import lax
from jax.experimental import pallas as pl
from jax.experimental.pallas import tpu as pltpu
from jax.sharding import Mesh
from jax.sharding import PartitionSpec as P


AX = ("xh", "core", "z", "xl", "y")
SIZES = (2, 2, 8, 2, 4)
WEIGHT_GROUP = ("z", "xl")
FSDP = ("z", "xl", "y")
GROUP_WIDTH = 24
OWN = 96
PIX = 1024
SIDE = 32
TAPS = 9
PAIR = 2 * OWN
QUAD = 4 * OWN
LANES = TAPS * PAIR
EPS = 1e-05
F32 = jnp.float32
BF16 = jnp.bfloat16


def flat(xh, core, z, xl, y):
    return (((xh * 2 + core) * 8 + z) * 2 + xl) * 4 + y


def every():
    for xh in range(2):
        for core in range(2):
            for z in range(8):
                for xl in range(2):
                    for y in range(4):
                        yield xh, core, z, xl, y


def pixel_pairs(turn, ahead):
    pairs = []
    for xh, core, z, xl, y in every():
        slot = ((z * 2 + xl) * 4 + y + ahead) % 64
        sample, piece = slot // 4, slot % 4
        u = (piece + turn) % 4
        pairs.append(
            (flat(xh, core, z, xl, y), flat(xh, u % 2, sample // 2, sample % 2, 2 * core + u // 2))
        )
    return pairs


def weight_pairs(second):
    pairs = []
    for xh, core, z, xl, y in every():
        b = (y & 1) ^ second
        if xh == 0:
            target = (0, z % 2, 2 * (z // 2) + xl, y >> 1, 2 * core + b)
        else:
            far = 2 * core + (y >> 1)
            target = (1, b, (z + (far if z % 2 else -far)) % 8, xl, z // 2)
        pairs.append((flat(xh, core, z, xl, y), flat(*target)))
    return pairs


def back(pairs):
    return [(b, a) for a, b in pairs]


def swap(value, axis):
    return lax.ppermute(value, axis, [(0, 1), (1, 0)])


def turn_y(value, d):
    return lax.ppermute(value, "y", [(i, (i + d) % 4) for i in range(4)])


def pixels():
    p = lax.broadcasted_iota(jnp.int32, (1, PIX), 1)
    return p >> 5, p & 31


def live(prm):
    row, col = pixels()
    return ((row < prm[3]) & (col < prm[4])).astype(F32)


def offsets(tap):
    return tap // 3 - 1, tap % 3 - 1


def moved(field, dr, dc):
    off = dr * SIDE + dc
    if off == 0:
        return field
    row, col = pixels()
    ok = (row + dr >= 0) & (row + dr < SIDE) & (col + dc >= 0) & (col + dc < SIDE)
    return pltpu.roll(field, (-off) % PIX, 1) * ok.astype(F32).astype(field.dtype)


def group_sum(field):
    return jnp.sum(field.reshape(OWN // GROUP_WIDTH, GROUP_WIDTH, PIX), axis=(1, 2), keepdims=True)


def spread(stat):
    return jnp.broadcast_to(stat, (OWN // GROUP_WIDTH, GROUP_WIDTH, PIX)).reshape(OWN, PIX)


def normed_of(values, mask, count):
    masked = values * mask
    mean = group_sum(masked) / count
    var = group_sum(masked * masked) / count - mean * mean
    scale = spread(lax.rsqrt(var + EPS))
    return (values - spread(mean)) * scale, scale


def count_of(prm):
    return (prm[3] * prm[4] * GROUP_WIDTH).astype(F32)


def silu_slope(u, s):
    return s * (1.0 + u * (1.0 - s))


def input_slope(e, xhat, scale, mask, count):
    m1 = spread(group_sum(e) / count)
    m2 = spread(group_sum(e * xhat) / count)
    return mask * (e - m1 - xhat * m2) * scale


def rows(k, n=OWN):
    return pl.ds(pl.multiple_of(k * n, n), n)


def split_kernel(prm, x_ref, *refs):
    outs, scratch = refs[:4], refs[4]
    scratch[...] = x_ref[...].astype(F32).T.astype(BF16)
    for v in range(4):
        outs[v][...] = scratch[rows((prm[2] + v) % 4), :]


def join_kernel(prm, *refs):
    ins, out, scratch = refs[:4], refs[4], refs[5]
    for v in range(4):
        scratch[rows((prm[5] + v) % 4), :] = ins[v][...]
    out[...] = scratch[...].astype(F32).T.astype(BF16)


def start_kernel(prm, *refs):
    ins, x_out, a_out = refs[:4], refs[4], refs[5]
    u = 2 * (prm[2] % 2) + prm[1]
    for v in range(4):
        t = (u - v + 4) % 4
        x_out[:, pl.ds(pl.multiple_of(t * 256, 256), 256)] = ins[v][...]
    mask = live(prm)
    values = x_out[...].astype(F32) * mask
    xhat, _ = normed_of(values, mask, count_of(prm))
    act = mask * (xhat * jax.nn.sigmoid(xhat))
    a_out[...] = jnp.where(prm[0] == 0, act, values).astype(BF16)


def convolve(w, act):
    acc = jnp.zeros((PAIR, PIX), F32)
    for tap in range(0, TAPS, 2):
        n = min(2, TAPS - tap)
        part = lax.dot_general(
            w[:, tap * PAIR : (tap + n) * PAIR],
            act,
            (((0,), (0,)), ((), ())),
            preferred_element_type=F32,
        )
        for k in range(n):
            acc = acc + moved(part[k * PAIR : (k + 1) * PAIR], *offsets(tap + k))
    return acc


def build_moved(act, d_ref):
    for tap in range(TAPS):
        dr, dc = offsets(tap)
        d_ref[tap * PAIR : (tap + 1) * PAIR, :] = moved(act, -dr, -dc)


def gather_chunks(prm, own, others, full):
    full[rows(prm[2]), :] = own[...]
    for d, ref in enumerate(others, 1):
        full[rows((prm[2] + 4 - d) % 4), :] = ref[...]


def parts_in_order(prm):
    for k in range(16):
        far, odd, xl = 2 * (k >> 3) + (k & 1), (k >> 2) & 1, (k >> 1) & 1
        plane = (2 * prm[2] + (1 + far if odd else 8 - far)) % 8
        yield k, rows(2 * plane + xl, 24)


def first_kernel(prm, w, g, a0, a1, a2, a3, full, keep, send, sorted_w, d_ref, res):
    gather_chunks(prm, a0, (a1, a2, a3), full)

    @pl.when(prm[0] == 0)
    def _():
        res[...] = convolve(w[...], full[...])

    @pl.when(prm[0] == 1)
    def _():
        for k, place in parts_in_order(prm):
            sorted_w[k * 24 : (k + 1) * 24, :] = w[place, :]
        for k in range(2):
            build_moved(full[k * PAIR : (k + 1) * PAIR, :], d_ref)
            part = jnp.dot(
                sorted_w[k * PAIR : (k + 1) * PAIR, :], d_ref[...], preferred_element_type=F32
            )
            if k == 0:
                res[...] = part
            else:
                res[...] += part

    keep[...] = res[rows(prm[1]), :]
    send[...] = res[rows(1 - prm[1]), :]


def middle_kernel(prm, x, keep, got, out):
    mask = live(prm)
    total = keep[...] + got[...]
    values = x[...].astype(F32) * mask
    out[...] = jnp.where(prm[0] == 0, values + mask * total, total).astype(BF16)


def turn_kernel(prm, mine, theirs, g, b_out, q_out):
    mask = live(prm)
    count = count_of(prm)
    down = prm[0] == 0
    hidden = jnp.where(down, mine[...].astype(F32), theirs[...].astype(F32))
    xhat, scale = normed_of(hidden, mask, count)
    s = jax.nn.sigmoid(xhat)

    @pl.when(down)
    def _():
        e = mask * theirs[...].astype(F32) * silu_slope(xhat, s)
        dv = (g[...].astype(F32) + input_slope(e, xhat, scale, mask, count)).astype(BF16)
        q_out[...] = dv
        b_out[...] = (dv.astype(F32) * mask).astype(BF16)

    @pl.when(jnp.logical_not(down))
    def _():
        q_out[...] = theirs[...]
        b_out[...] = (mask * (xhat * s)).astype(BF16)


def pair_up(prm, own, other, pair):
    pair[rows(prm[1]), :] = own[...]
    pair[rows(1 - prm[1]), :] = other[...]


def weight_slope_kernel(prm, full, b_own, b_other, dw, pair, d_ref):
    pair_up(prm, b_own, b_other, pair)

    def product(lhs):
        return lax.dot_general(
            lhs, d_ref[...], (((1,), (1,)), ((), ())), preferred_element_type=F32
        )

    @pl.when(prm[0] == 0)
    def _():
        build_moved(pair[...], d_ref)
        dw[...] = product(full[...]).astype(BF16)

    @pl.when(prm[0] == 1)
    def _():
        for k in range(2):
            build_moved(full[k * PAIR : (k + 1) * PAIR, :], d_ref)
            part = product(pair[...])
            for m, place in parts_in_order(prm):
                if m // 8 == k:
                    dw[place, :] = part[m % 8 * 24 : (m % 8 + 1) * 24, :].astype(BF16)


def second_kernel(prm, w, sorted_w, b_own, b_other, keep, s1, s2, s3, pair, d_ref, res):
    pair_up(prm, b_own, b_other, pair)

    @pl.when(prm[0] == 0)
    def _():
        build_moved(pair[...], d_ref)
        res[...] = jnp.dot(w[...], d_ref[...], preferred_element_type=F32)

    @pl.when(prm[0] == 1)
    def _():
        for k in range(2):
            res[k * PAIR : (k + 1) * PAIR, :] = convolve(
                sorted_w[k * PAIR : (k + 1) * PAIR, :], pair[...]
            )

    keep[...] = res[rows(prm[2]), :]
    for d, ref in enumerate((s1, s2, s3), 1):
        ref[...] = res[rows((prm[2] + d) % 4), :].astype(BF16)


def last_kernel(prm, x, q, keep, r1, r2, r3, *refs):
    outs, scratch = refs[:4], refs[4]
    mask = live(prm)
    count = count_of(prm)
    total = keep[...] + r1[...].astype(F32) + r2[...].astype(F32) + r3[...].astype(F32)
    carried = q[...].astype(F32)

    @pl.when(prm[0] == 0)
    def _():
        xhat, scale = normed_of(x[...].astype(F32) * mask, mask, count)
        e = mask * total * silu_slope(xhat, jax.nn.sigmoid(xhat))
        slope = input_slope(e, xhat, scale, mask, count)
        scratch[...] = (mask * (carried + slope)).astype(BF16)

    @pl.when(prm[0] == 1)
    def _():
        scratch[...] = (carried + mask * total).astype(BF16)

    u = 2 * (prm[2] % 2) + prm[1]
    for v in range(4):
        t = (u - v + 4) % 4
        outs[v][...] = scratch[:, pl.ds(pl.multiple_of(t * 256, 256), 256)]


def call(kernel, outs, scratch, prm, *args, grant=8):
    vmem = pl.BlockSpec(memory_space=pltpu.VMEM)
    return pl.pallas_call(
        kernel,
        out_shape=[jax.ShapeDtypeStruct(s, d) for s, d in outs],
        in_specs=[pl.BlockSpec(memory_space=pltpu.SMEM)] + [vmem] * len(args),
        out_specs=[vmem] * len(outs),
        scratch_shapes=[pltpu.VMEM(s, d) for s, d in scratch],
        compiler_params=pltpu.CompilerParams(vmem_limit_bytes=grant << 20),
    )(prm, *args)


def step(signals, conv_weight, buckets):
    xh, core, z, _, y = (lax.axis_index(a) for a in AX)
    micro = z // 4
    own_bucket = jnp.where(micro == 0, buckets[0], buckets[1])
    size = 16 + 2 * own_bucket
    piece = (y + 1) % 4
    prm = jnp.stack([xh, core, y, size[0], size[1], piece]).astype(jnp.int32)
    own = ((OWN, PIX), BF16)
    own32 = ((OWN, PIX), F32)

    cut = conv_weight.reshape(12, TAPS, 4, OWN)
    low = jnp.where(xh == 0, cut[:, :, 0:2], cut[:, :, 0::2]).reshape(12, LANES)
    high = jnp.where(xh == 0, cut[:, :, 2:4], cut[:, :, 1::2]).reshape(12, LANES)
    odd = y % 2 == 1
    got = [
        lax.ppermute(jnp.where(odd, high, low), AX, weight_pairs(0)),
        lax.ppermute(jnp.where(odd, low, high), AX, weight_pairs(1)),
    ]
    flip = jnp.where(xh == 0, y % 2, core) == 1
    part = jnp.concatenate([jnp.where(flip, got[1], got[0]), jnp.where(flip, got[0], got[1])], 0)
    copies = jnp.broadcast_to(part, (16, 24, LANES))
    w = lax.all_to_all(copies, WEIGHT_GROUP, 0, 0, tiled=True).reshape(QUAD, LANES)

    shifted = lax.ppermute(signals, FSDP, [(i, (i + 1) % 64) for i in range(64)])
    blocks = call(
        split_kernel, [((OWN, 256), BF16)] * 4, [((QUAD, 256), BF16)], prm, shifted
    )
    blocks = [lax.ppermute(b, AX, pixel_pairs(v, 0)) for v, b in enumerate(blocks)]
    x, a = call(start_kernel, [own, own], [], prm, *blocks)
    others = [turn_y(a, d) for d in (1, 2, 3)]
    g = swap(x, "xh")

    full, keep, send, sorted_w = call(
        first_kernel,
        [((QUAD, PIX), BF16), own32, own32, ((QUAD, LANES), BF16)],
        [((LANES, PIX), BF16), ((PAIR, PIX), F32)],
        prm,
        w,
        g,
        a,
        *others,
        grant=24,
    )
    (mine,) = call(middle_kernel, [own], [], prm, x, keep, swap(send, "core"))
    theirs = swap(mine, "xh")
    b, q = call(turn_kernel, [own, own], [], prm, mine, theirs, g)
    b_other = swap(b, "core")
    (dw,) = call(
        weight_slope_kernel,
        [((QUAD, LANES), BF16)],
        [((PAIR, PIX), BF16), ((LANES, PIX), BF16)],
        prm,
        full,
        b,
        b_other,
        grant=24,
    )
    keep, *sends = call(
        second_kernel,
        [own32, own, own, own],
        [((PAIR, PIX), BF16), ((LANES, PIX), BF16), ((QUAD, PIX), F32)],
        prm,
        w,
        sorted_w,
        b,
        b_other,
        grant=24,
    )
    got = [turn_y(s, d) for d, s in enumerate(sends, 1)]
    blocks = call(last_kernel, [((OWN, 256), BF16)] * 4, [own], prm, x, q, keep, *got)
    blocks = [lax.ppermute(b, AX, back(pixel_pairs(v, 1))) for v, b in enumerate(blocks)]
    (results,) = call(
        join_kernel, [((256, QUAD), BF16)], [((QUAD, 256), BF16)], prm, *blocks
    )

    shares = lax.all_to_all(dw.reshape(16, 24, LANES), WEIGHT_GROUP, 0, 0, tiled=True)
    total = jnp.sum(shares.astype(F32), axis=0).astype(BF16)
    first, second = total[:12], total[12:]
    low_high = [
        lax.ppermute(jnp.where(flip, second, first), AX, back(weight_pairs(0))),
        lax.ppermute(jnp.where(flip, first, second), AX, back(weight_pairs(1))),
    ]
    low = jnp.where(odd, low_high[1], low_high[0]).reshape(12, TAPS, 2, OWN)
    high = jnp.where(odd, low_high[0], low_high[1]).reshape(12, TAPS, 2, OWN)
    apart = jnp.concatenate([low, high], axis=2)
    woven = jnp.stack([low, high], axis=3).reshape(12, TAPS, 4, OWN)
    grad_weight = jnp.where(xh == 0, apart, woven).reshape(12, TAPS, QUAD).astype(F32)
    return results, grad_weight


def solution(mesh):
    finer = Mesh(mesh.devices.reshape(SIZES), AX)
    section, fsdp = ("xh", "core"), ("z", "xl", "y")
    placed = (P(fsdp, section), P(fsdp, None, section), P())
    return jax.shard_map(
        step,
        mesh=finer,
        in_specs=placed,
        out_specs=(P(fsdp, section), P(fsdp, None, section)),
        check_vma=False,
    )
```

```python
import jax
import jax.numpy as jnp
from jax import lax
from jax.experimental import pallas as pl
from jax.experimental.pallas import tpu as pltpu
from jax.sharding import Mesh
from jax.sharding import PartitionSpec as P


AX = ("xh", "core", "z", "xl", "y")
SIZES = (2, 2, 8, 2, 4)
WEIGHT_GROUP = ("z", "xl")
FSDP = ("z", "xl", "y")
GROUP_WIDTH = 24
OWN = 96
PIX = 1024
SIDE = 32
TAPS = 9
PAIR = 2 * OWN
QUAD = 4 * OWN
LANES = TAPS * PAIR
EPS = 1e-05
F32 = jnp.float32
BF16 = jnp.bfloat16


def flat(xh, core, z, xl, y):
    return (((xh * 2 + core) * 8 + z) * 2 + xl) * 4 + y


def every():
    for xh in range(2):
        for core in range(2):
            for z in range(8):
                for xl in range(2):
                    for y in range(4):
                        yield xh, core, z, xl, y


def pixel_pairs(turn, ahead):
    pairs = []
    for xh, core, z, xl, y in every():
        slot = ((z * 2 + xl) * 4 + y + ahead) % 64
        sample, piece = slot // 4, slot % 4
        u = (piece + turn) % 4
        pairs.append(
            (flat(xh, core, z, xl, y), flat(xh, u % 2, sample // 2, sample % 2, 2 * core + u // 2))
        )
    return pairs


def weight_pairs(second):
    pairs = []
    for xh, core, z, xl, y in every():
        b = (y & 1) ^ second
        if xh == 0:
            target = (0, z % 2, 2 * (z // 2) + xl, y >> 1, 2 * core + b)
        else:
            far = 2 * core + (y >> 1)
            target = (1, b, (z + (far if z % 2 else -far)) % 8, xl, z // 2)
        pairs.append((flat(xh, core, z, xl, y), flat(*target)))
    return pairs


def back(pairs):
    return [(b, a) for a, b in pairs]


def swap(value, axis):
    return lax.ppermute(value, axis, [(0, 1), (1, 0)])


def turn_y(value, d):
    return lax.ppermute(value, "y", [(i, (i + d) % 4) for i in range(4)])


def pixels():
    p = lax.broadcasted_iota(jnp.int32, (1, PIX), 1)
    return p >> 5, p & 31


def live(prm):
    row, col = pixels()
    return ((row < prm[3]) & (col < prm[4])).astype(F32)


def offsets(tap):
    return tap // 3 - 1, tap % 3 - 1


def moved(field, dr, dc):
    off = dr * SIDE + dc
    if off == 0:
        return field
    row, col = pixels()
    ok = (row + dr >= 0) & (row + dr < SIDE) & (col + dc >= 0) & (col + dc < SIDE)
    return pltpu.roll(field, (-off) % PIX, 1) * ok.astype(F32).astype(field.dtype)


def group_sum(field):
    return jnp.sum(field.reshape(OWN // GROUP_WIDTH, GROUP_WIDTH, PIX), axis=(1, 2), keepdims=True)


def spread(stat):
    return jnp.broadcast_to(stat, (OWN // GROUP_WIDTH, GROUP_WIDTH, PIX)).reshape(OWN, PIX)


def normed_of(values, mask, count):
    masked = values * mask
    mean = group_sum(masked) / count
    var = group_sum(masked * masked) / count - mean * mean
    scale = spread(lax.rsqrt(var + EPS))
    return (values - spread(mean)) * scale, scale


def count_of(prm):
    return (prm[3] * prm[4] * GROUP_WIDTH).astype(F32)


def silu_slope(u, s):
    return s * (1.0 + u * (1.0 - s))


def input_slope(e, xhat, scale, mask, count):
    m1 = spread(group_sum(e) / count)
    m2 = spread(group_sum(e * xhat) / count)
    return mask * (e - m1 - xhat * m2) * scale


def rows(k, n=OWN):
    return pl.ds(pl.multiple_of(k * n, n), n)


def split_kernel(prm, x_ref, *refs):
    outs, scratch = refs[:4], refs[4]
    scratch[...] = x_ref[...].astype(F32).T.astype(BF16)
    for v in range(4):
        outs[v][...] = scratch[rows((prm[2] + v) % 4), :]


def join_kernel(prm, *refs):
    ins, out, scratch = refs[:4], refs[4], refs[5]
    for v in range(4):
        scratch[rows((prm[5] + v) % 4), :] = ins[v][...]
    out[...] = scratch[...].astype(F32).T.astype(BF16)


def start_kernel(prm, *refs):
    ins, x_out, a_out = refs[:4], refs[4], refs[5]
    u = 2 * (prm[2] % 2) + prm[1]
    for v in range(4):
        t = (u - v + 4) % 4
        x_out[:, pl.ds(pl.multiple_of(t * 256, 256), 256)] = ins[v][...]
    mask = live(prm)
    values = x_out[...].astype(F32) * mask
    xhat, _ = normed_of(values, mask, count_of(prm))
    act = mask * (xhat * jax.nn.sigmoid(xhat))
    a_out[...] = jnp.where(prm[0] == 0, act, values).astype(BF16)


def convolve(w, act):
    acc = jnp.zeros((PAIR, PIX), F32)
    for tap in range(0, TAPS, 2):
        n = min(2, TAPS - tap)
        part = lax.dot_general(
            w[:, tap * PAIR : (tap + n) * PAIR],
            act,
            (((0,), (0,)), ((), ())),
            preferred_element_type=F32,
        )
        for k in range(n):
            acc = acc + moved(part[k * PAIR : (k + 1) * PAIR], *offsets(tap + k))
    return acc


def build_moved(act, d_ref):
    for tap in range(TAPS):
        dr, dc = offsets(tap)
        d_ref[tap * PAIR : (tap + 1) * PAIR, :] = moved(act, -dr, -dc)


def gather_chunks(prm, own, others, full):
    full[rows(prm[2]), :] = own[...]
    for d, ref in enumerate(others, 1):
        full[rows((prm[2] + 4 - d) % 4), :] = ref[...]


def parts_in_order(prm):
    for k in range(16):
        far, odd, xl = 2 * (k >> 3) + (k & 1), (k >> 2) & 1, (k >> 1) & 1
        plane = (2 * prm[2] + (1 + far if odd else 8 - far)) % 8
        yield k, rows(2 * plane + xl, 24)


def first_kernel(prm, w, a0, a1, a2, a3, full, keep, send, sorted_w, d_ref, res):
    gather_chunks(prm, a0, (a1, a2, a3), full)

    @pl.when(prm[0] == 0)
    def _():
        res[...] = convolve(w[...], full[...])

    @pl.when(prm[0] == 1)
    def _():
        for k, place in parts_in_order(prm):
            sorted_w[k * 24 : (k + 1) * 24, :] = w[place, :]
        for k in range(2):
            build_moved(full[k * PAIR : (k + 1) * PAIR, :], d_ref)
            part = jnp.dot(
                sorted_w[k * PAIR : (k + 1) * PAIR, :], d_ref[...], preferred_element_type=F32
            )
            if k == 0:
                res[...] = part
            else:
                res[...] += part

    keep[...] = res[rows(prm[1]), :]
    send[...] = res[rows(1 - prm[1]), :]


def middle_kernel(prm, x, keep, got, out):
    mask = live(prm)
    total = keep[...] + got[...]
    values = x[...].astype(F32) * mask
    out[...] = jnp.where(prm[0] == 0, values + mask * total, total).astype(BF16)


def turn_kernel(prm, mine, theirs, g, b_out, q_out):
    mask = live(prm)
    count = count_of(prm)
    down = prm[0] == 0
    hidden = jnp.where(down, mine[...].astype(F32), theirs[...].astype(F32))
    xhat, scale = normed_of(hidden, mask, count)
    s = jax.nn.sigmoid(xhat)

    @pl.when(down)
    def _():
        e = mask * theirs[...].astype(F32) * silu_slope(xhat, s)
        dv = (g[...].astype(F32) + input_slope(e, xhat, scale, mask, count)).astype(BF16)
        q_out[...] = dv
        b_out[...] = (dv.astype(F32) * mask).astype(BF16)

    @pl.when(jnp.logical_not(down))
    def _():
        q_out[...] = theirs[...]
        b_out[...] = (mask * (xhat * s)).astype(BF16)


def pair_up(prm, own, other, pair):
    pair[rows(prm[1]), :] = own[...]
    pair[rows(1 - prm[1]), :] = other[...]


def weight_slope_kernel(prm, full, b_own, b_other, dw, pair, d_ref):
    pair_up(prm, b_own, b_other, pair)

    def product(lhs):
        return lax.dot_general(
            lhs, d_ref[...], (((1,), (1,)), ((), ())), preferred_element_type=F32
        )

    @pl.when(prm[0] == 0)
    def _():
        build_moved(pair[...], d_ref)
        dw[...] = product(full[...]).astype(BF16)

    @pl.when(prm[0] == 1)
    def _():
        for k in range(2):
            build_moved(full[k * PAIR : (k + 1) * PAIR, :], d_ref)
            part = product(pair[...])
            for m, place in parts_in_order(prm):
                if m // 8 == k:
                    dw[place, :] = part[m % 8 * 24 : (m % 8 + 1) * 24, :].astype(BF16)


def second_kernel(prm, w, b_own, b_other, keep, s1, s2, s3, sorted_w, pair, d_ref, res):
    pair_up(prm, b_own, b_other, pair)

    @pl.when(prm[0] == 0)
    def _():
        build_moved(pair[...], d_ref)
        res[...] = jnp.dot(w[...], d_ref[...], preferred_element_type=F32)

    @pl.when(prm[0] == 1)
    def _():
        for k, place in parts_in_order(prm):
            sorted_w[k * 24 : (k + 1) * 24, :] = w[place, :]
        for k in range(2):
            res[k * PAIR : (k + 1) * PAIR, :] = convolve(
                sorted_w[k * PAIR : (k + 1) * PAIR, :], pair[...]
            )

    keep[...] = res[rows(prm[2]), :]
    for d, ref in enumerate((s1, s2, s3), 1):
        ref[...] = res[rows((prm[2] + d) % 4), :].astype(BF16)


def last_kernel(prm, x, q, keep, r1, r2, r3, *refs):
    outs, scratch = refs[:4], refs[4]
    mask = live(prm)
    count = count_of(prm)
    total = keep[...] + r1[...].astype(F32) + r2[...].astype(F32) + r3[...].astype(F32)
    carried = q[...].astype(F32)

    @pl.when(prm[0] == 0)
    def _():
        xhat, scale = normed_of(x[...].astype(F32) * mask, mask, count)
        e = mask * total * silu_slope(xhat, jax.nn.sigmoid(xhat))
        slope = input_slope(e, xhat, scale, mask, count)
        scratch[...] = (mask * (carried + slope)).astype(BF16)

    @pl.when(prm[0] == 1)
    def _():
        scratch[...] = (carried + mask * total).astype(BF16)

    u = 2 * (prm[2] % 2) + prm[1]
    for v in range(4):
        t = (u - v + 4) % 4
        outs[v][...] = scratch[:, pl.ds(pl.multiple_of(t * 256, 256), 256)]


def call(kernel, outs, scratch, prm, *args, grant=8):
    vmem = pl.BlockSpec(memory_space=pltpu.VMEM)
    return pl.pallas_call(
        kernel,
        out_shape=[jax.ShapeDtypeStruct(s, d) for s, d in outs],
        in_specs=[pl.BlockSpec(memory_space=pltpu.SMEM)] + [vmem] * len(args),
        out_specs=[vmem] * len(outs),
        scratch_shapes=[pltpu.VMEM(s, d) for s, d in scratch],
        compiler_params=pltpu.CompilerParams(vmem_limit_bytes=grant << 20),
    )(prm, *args)


def step(signals, conv_weight, buckets):
    xh, core, z, _, y = (lax.axis_index(a) for a in AX)
    micro = z // 4
    own_bucket = jnp.where(micro == 0, buckets[0], buckets[1])
    size = 16 + 2 * own_bucket
    piece = (y + 1) % 4
    prm = jnp.stack([xh, core, y, size[0], size[1], piece]).astype(jnp.int32)
    own = ((OWN, PIX), BF16)
    own32 = ((OWN, PIX), F32)

    cut = conv_weight.reshape(12, TAPS, 4, OWN)
    low = jnp.where(xh == 0, cut[:, :, 0:2], cut[:, :, 0::2]).reshape(12, LANES)
    high = jnp.where(xh == 0, cut[:, :, 2:4], cut[:, :, 1::2]).reshape(12, LANES)
    odd = y % 2 == 1
    got = [
        lax.ppermute(jnp.where(odd, high, low), AX, weight_pairs(0)),
        lax.ppermute(jnp.where(odd, low, high), AX, weight_pairs(1)),
    ]
    flip = jnp.where(xh == 0, y % 2, core) == 1
    part = jnp.concatenate([jnp.where(flip, got[1], got[0]), jnp.where(flip, got[0], got[1])], 0)
    copies = jnp.broadcast_to(part, (16, 24, LANES))
    w = lax.all_to_all(copies, WEIGHT_GROUP, 0, 0, tiled=True).reshape(QUAD, LANES)

    shifted = lax.ppermute(signals, FSDP, [(i, (i + 1) % 64) for i in range(64)])
    blocks = call(
        split_kernel, [((OWN, 256), BF16)] * 4, [((QUAD, 256), BF16)], prm, shifted
    )
    blocks = [lax.ppermute(b, AX, pixel_pairs(v, 0)) for v, b in enumerate(blocks)]
    x, a = call(start_kernel, [own, own], [], prm, *blocks)
    others = [turn_y(a, d) for d in (1, 2, 3)]
    g = swap(x, "xh")

    full, keep, send = call(
        first_kernel,
        [((QUAD, PIX), BF16), own32, own32],
        [((QUAD, LANES), BF16), ((LANES, PIX), BF16), ((PAIR, PIX), F32)],
        prm,
        w,
        a,
        *others,
        grant=24,
    )
    (mine,) = call(middle_kernel, [own], [], prm, x, keep, swap(send, "core"))
    theirs = swap(mine, "xh")
    b, q = call(turn_kernel, [own, own], [], prm, mine, theirs, g)
    b_other = swap(b, "core")
    (dw,) = call(
        weight_slope_kernel,
        [((QUAD, LANES), BF16)],
        [((PAIR, PIX), BF16), ((LANES, PIX), BF16)],
        prm,
        full,
        b,
        b_other,
        grant=24,
    )
    keep, *sends = call(
        second_kernel,
        [own32, own, own, own],
        [
            ((QUAD, LANES), BF16),
            ((PAIR, PIX), BF16),
            ((LANES, PIX), BF16),
            ((QUAD, PIX), F32),
        ],
        prm,
        w,
        b,
        b_other,
        grant=24,
    )
    got = [turn_y(s, d) for d, s in enumerate(sends, 1)]
    blocks = call(last_kernel, [((OWN, 256), BF16)] * 4, [own], prm, x, q, keep, *got)
    blocks = [lax.ppermute(b, AX, back(pixel_pairs(v, 1))) for v, b in enumerate(blocks)]
    (results,) = call(
        join_kernel, [((256, QUAD), BF16)], [((QUAD, 256), BF16)], prm, *blocks
    )

    shares = lax.all_to_all(dw.reshape(16, 24, LANES), WEIGHT_GROUP, 0, 0, tiled=True)
    total = jnp.sum(shares.astype(F32), axis=0).astype(BF16)
    first, second = total[:12], total[12:]
    low_high = [
        lax.ppermute(jnp.where(flip, second, first), AX, back(weight_pairs(0))),
        lax.ppermute(jnp.where(flip, first, second), AX, back(weight_pairs(1))),
    ]
    low = jnp.where(odd, low_high[1], low_high[0]).reshape(12, TAPS, 2, OWN)
    high = jnp.where(odd, low_high[0], low_high[1]).reshape(12, TAPS, 2, OWN)
    apart = jnp.concatenate([low, high], axis=2)
    woven = jnp.stack([low, high], axis=3).reshape(12, TAPS, 4, OWN)
    grad_weight = jnp.where(xh == 0, apart, woven).reshape(12, TAPS, QUAD).astype(F32)
    return results, grad_weight


def solution(mesh):
    finer = Mesh(mesh.devices.reshape(SIZES), AX)
    section, fsdp = ("xh", "core"), ("z", "xl", "y")
    placed = (P(fsdp, section), P(fsdp, None, section), P())
    return jax.shard_map(
        step,
        mesh=finer,
        in_specs=placed,
        out_specs=(P(fsdp, section), P(fsdp, None, section)),
        check_vma=False,
    )
```

```python
import jax
import jax.numpy as jnp
from jax import lax
from jax.experimental import pallas as pl
from jax.experimental.pallas import tpu as pltpu
from jax.sharding import Mesh
from jax.sharding import PartitionSpec as P


AX = ("xh", "core", "z", "xl", "y")
SIZES = (2, 2, 8, 2, 4)
WEIGHT_GROUP = ("z", "xl")
FSDP = ("z", "xl", "y")
GROUP_WIDTH = 24
OWN = 96
PIX = 1024
SIDE = 32
TAPS = 9
PAIR = 2 * OWN
QUAD = 4 * OWN
LANES = TAPS * PAIR
EPS = 1e-05
F32 = jnp.float32
BF16 = jnp.bfloat16


def flat(xh, core, z, xl, y):
    return (((xh * 2 + core) * 8 + z) * 2 + xl) * 4 + y


def every():
    for xh in range(2):
        for core in range(2):
            for z in range(8):
                for xl in range(2):
                    for y in range(4):
                        yield xh, core, z, xl, y


def pixel_pairs(turn):
    pairs = []
    for xh, core, z, xl, y in every():
        u = (y + turn) % 4
        pairs.append((flat(xh, core, z, xl, y), flat(xh, u % 2, z, xl, 2 * core + u // 2)))
    return pairs


def weight_pairs(second):
    pairs = []
    for xh, core, z, xl, y in every():
        b = (y & 1) ^ second
        if xh == 0:
            target = (0, z % 2, 2 * (z // 2) + xl, y >> 1, 2 * core + b)
        else:
            far = 2 * core + (y >> 1)
            target = (1, b, (z + (far if z % 2 else -far)) % 8, xl, z // 2)
        pairs.append((flat(xh, core, z, xl, y), flat(*target)))
    return pairs


def back(pairs):
    return [(b, a) for a, b in pairs]


def swap(value, axis):
    return lax.ppermute(value, axis, [(0, 1), (1, 0)])


def turn_y(value, d):
    return lax.ppermute(value, "y", [(i, (i + d) % 4) for i in range(4)])


def shift(value, d):
    return lax.ppermute(value, FSDP, [(i, (i + d) % 64) for i in range(64)])


def pixels():
    p = lax.broadcasted_iota(jnp.int32, (1, PIX), 1)
    return p >> 5, p & 31


def live(prm):
    row, col = pixels()
    return ((row < prm[3]) & (col < prm[4])).astype(F32)


def offsets(tap):
    return tap // 3 - 1, tap % 3 - 1


def moved(field, dr, dc):
    off = dr * SIDE + dc
    if off == 0:
        return field
    row, col = pixels()
    ok = (row + dr >= 0) & (row + dr < SIDE) & (col + dc >= 0) & (col + dc < SIDE)
    return pltpu.roll(field, (-off) % PIX, 1) * ok.astype(F32).astype(field.dtype)


def group_sum(field):
    return jnp.sum(field.reshape(OWN // GROUP_WIDTH, GROUP_WIDTH, PIX), axis=(1, 2), keepdims=True)


def spread(stat):
    return jnp.broadcast_to(stat, (OWN // GROUP_WIDTH, GROUP_WIDTH, PIX)).reshape(OWN, PIX)


def normed_of(values, mask, count):
    masked = values * mask
    mean = group_sum(masked) / count
    var = group_sum(masked * masked) / count - mean * mean
    scale = spread(lax.rsqrt(var + EPS))
    return (values - spread(mean)) * scale, scale


def count_of(prm):
    return (prm[3] * prm[4] * GROUP_WIDTH).astype(F32)


def silu_slope(u, s):
    return s * (1.0 + u * (1.0 - s))


def input_slope(e, xhat, scale, mask, count):
    m1 = spread(group_sum(e) / count)
    m2 = spread(group_sum(e * xhat) / count)
    return mask * (e - m1 - xhat * m2) * scale


def rows(k, n=OWN):
    return pl.ds(pl.multiple_of(k * n, n), n)


def split_kernel(prm, x_ref, *refs):
    outs, scratch = refs[:4], refs[4]
    scratch[...] = x_ref[...].astype(F32).T.astype(BF16)
    for v in range(4):
        outs[v][...] = scratch[rows((prm[2] + v) % 4), :]


def join_kernel(prm, *refs):
    ins, out, scratch = refs[:4], refs[4], refs[5]
    for v in range(4):
        scratch[rows((prm[2] + v) % 4), :] = ins[v][...]
    out[...] = scratch[...].astype(F32).T.astype(BF16)


def start_kernel(prm, *refs):
    ins, x_out, a_out = refs[:4], refs[4], refs[5]
    u = 2 * (prm[2] % 2) + prm[1]
    for v in range(4):
        t = (u - v + 4) % 4
        x_out[:, pl.ds(pl.multiple_of(t * 256, 256), 256)] = ins[v][...]
    mask = live(prm)
    values = x_out[...].astype(F32) * mask
    xhat, _ = normed_of(values, mask, count_of(prm))
    act = mask * (xhat * jax.nn.sigmoid(xhat))
    a_out[...] = jnp.where(prm[0] == 0, act, values).astype(BF16)


def convolve(w, act):
    acc = jnp.zeros((PAIR, PIX), F32)
    for tap in range(0, TAPS, 2):
        n = min(2, TAPS - tap)
        part = lax.dot_general(
            w[:, tap * PAIR : (tap + n) * PAIR],
            act,
            (((0,), (0,)), ((), ())),
            preferred_element_type=F32,
        )
        for k in range(n):
            acc = acc + moved(part[k * PAIR : (k + 1) * PAIR], *offsets(tap + k))
    return acc


def build_moved(act, d_ref):
    for tap in range(TAPS):
        dr, dc = offsets(tap)
        d_ref[tap * PAIR : (tap + 1) * PAIR, :] = moved(act, -dr, -dc)


def gather_chunks(prm, own, others, full):
    full[rows(prm[2]), :] = own[...]
    for d, ref in enumerate(others, 1):
        full[rows((prm[2] + 4 - d) % 4), :] = ref[...]


def parts_in_order(prm):
    for k in range(16):
        far, odd, xl = 2 * (k >> 3) + (k & 1), (k >> 2) & 1, (k >> 1) & 1
        plane = (2 * prm[2] + (1 + far if odd else 8 - far)) % 8
        yield k, rows(2 * plane + xl, 24)


def first_kernel(prm, w, a0, a1, a2, a3, full, keep, send, sorted_w, d_ref, res):
    gather_chunks(prm, a0, (a1, a2, a3), full)

    @pl.when(prm[0] == 0)
    def _():
        res[...] = convolve(w[...], full[...])

    @pl.when(prm[0] == 1)
    def _():
        for k, place in parts_in_order(prm):
            sorted_w[k * 24 : (k + 1) * 24, :] = w[place, :]
        for k in range(2):
            build_moved(full[k * PAIR : (k + 1) * PAIR, :], d_ref)
            part = jnp.dot(
                sorted_w[k * PAIR : (k + 1) * PAIR, :], d_ref[...], preferred_element_type=F32
            )
            if k == 0:
                res[...] = part
            else:
                res[...] += part

    keep[...] = res[rows(prm[1]), :]
    send[...] = res[rows(1 - prm[1]), :]


def middle_kernel(prm, x, keep, got, out):
    mask = live(prm)
    total = keep[...] + got[...]
    values = x[...].astype(F32) * mask
    out[...] = jnp.where(prm[0] == 0, values + mask * total, total).astype(BF16)


def turn_kernel(prm, mine, theirs, g, b_out, q_out):
    mask = live(prm)
    count = count_of(prm)
    down = prm[0] == 0
    hidden = jnp.where(down, mine[...].astype(F32), theirs[...].astype(F32))
    xhat, scale = normed_of(hidden, mask, count)
    s = jax.nn.sigmoid(xhat)

    @pl.when(down)
    def _():
        e = mask * theirs[...].astype(F32) * silu_slope(xhat, s)
        dv = (g[...].astype(F32) + input_slope(e, xhat, scale, mask, count)).astype(BF16)
        q_out[...] = dv
        b_out[...] = (dv.astype(F32) * mask).astype(BF16)

    @pl.when(jnp.logical_not(down))
    def _():
        q_out[...] = theirs[...]
        b_out[...] = (mask * (xhat * s)).astype(BF16)


def pair_up(prm, own, other, pair):
    pair[rows(prm[1]), :] = own[...]
    pair[rows(1 - prm[1]), :] = other[...]


def weight_slope_kernel(prm, full, b_own, b_other, dw, pair, d_ref):
    pair_up(prm, b_own, b_other, pair)

    def product(lhs):
        return lax.dot_general(
            lhs, d_ref[...], (((1,), (1,)), ((), ())), preferred_element_type=F32
        )

    @pl.when(prm[0] == 0)
    def _():
        build_moved(pair[...], d_ref)
        dw[...] = product(full[...]).astype(BF16)

    @pl.when(prm[0] == 1)
    def _():
        for k in range(2):
            build_moved(full[k * PAIR : (k + 1) * PAIR, :], d_ref)
            part = product(pair[...])
            for m, place in parts_in_order(prm):
                if m // 8 == k:
                    dw[place, :] = part[m % 8 * 24 : (m % 8 + 1) * 24, :].astype(BF16)


def second_kernel(prm, w, b_own, b_other, keep, s1, s2, s3, sorted_w, pair, d_ref, res):
    pair_up(prm, b_own, b_other, pair)

    @pl.when(prm[0] == 0)
    def _():
        build_moved(pair[...], d_ref)
        res[...] = jnp.dot(w[...], d_ref[...], preferred_element_type=F32)

    @pl.when(prm[0] == 1)
    def _():
        for k, place in parts_in_order(prm):
            sorted_w[k * 24 : (k + 1) * 24, :] = w[place, :]
        for k in range(2):
            res[k * PAIR : (k + 1) * PAIR, :] = convolve(
                sorted_w[k * PAIR : (k + 1) * PAIR, :], pair[...]
            )

    keep[...] = res[rows(prm[2]), :]
    for d, ref in enumerate((s1, s2, s3), 1):
        ref[...] = res[rows((prm[2] + d) % 4), :].astype(BF16)


def last_kernel(prm, x, q, keep, r1, r2, r3, *refs):
    outs, scratch = refs[:4], refs[4]
    mask = live(prm)
    count = count_of(prm)
    total = keep[...] + r1[...].astype(F32) + r2[...].astype(F32) + r3[...].astype(F32)
    carried = q[...].astype(F32)

    @pl.when(prm[0] == 0)
    def _():
        xhat, scale = normed_of(x[...].astype(F32) * mask, mask, count)
        e = mask * total * silu_slope(xhat, jax.nn.sigmoid(xhat))
        slope = input_slope(e, xhat, scale, mask, count)
        scratch[...] = (mask * (carried + slope)).astype(BF16)

    @pl.when(prm[0] == 1)
    def _():
        scratch[...] = (carried + mask * total).astype(BF16)

    u = 2 * (prm[2] % 2) + prm[1]
    for v in range(4):
        t = (u - v + 4) % 4
        outs[v][...] = scratch[:, pl.ds(pl.multiple_of(t * 256, 256), 256)]


def call(kernel, outs, scratch, prm, *args, grant=8):
    vmem = pl.BlockSpec(memory_space=pltpu.VMEM)
    return pl.pallas_call(
        kernel,
        out_shape=[jax.ShapeDtypeStruct(s, d) for s, d in outs],
        in_specs=[pl.BlockSpec(memory_space=pltpu.SMEM)] + [vmem] * len(args),
        out_specs=[vmem] * len(outs),
        scratch_shapes=[pltpu.VMEM(s, d) for s, d in scratch],
        compiler_params=pltpu.CompilerParams(vmem_limit_bytes=grant << 20),
    )(prm, *args)


def step(signals, conv_weight, buckets):
    xh, core, z, _, y = (lax.axis_index(a) for a in AX)
    micro = z // 4
    own_bucket = jnp.where(micro == 0, buckets[0], buckets[1])
    size = 16 + 2 * own_bucket
    prm = jnp.stack([xh, core, y, size[0], size[1]]).astype(jnp.int32)
    own = ((OWN, PIX), BF16)
    own32 = ((OWN, PIX), F32)

    cut = conv_weight.reshape(12, TAPS, 4, OWN)
    low = jnp.where(xh == 0, cut[:, :, 0:2], cut[:, :, 0::2]).reshape(12, LANES)
    high = jnp.where(xh == 0, cut[:, :, 2:4], cut[:, :, 1::2]).reshape(12, LANES)
    odd = y % 2 == 1
    got = [
        lax.ppermute(jnp.where(odd, high, low), AX, weight_pairs(0)),
        lax.ppermute(jnp.where(odd, low, high), AX, weight_pairs(1)),
    ]
    flip = jnp.where(xh == 0, y % 2, core) == 1
    part = jnp.concatenate([jnp.where(flip, got[1], got[0]), jnp.where(flip, got[0], got[1])], 0)
    copies = jnp.broadcast_to(part, (16, 24, LANES))
    w = lax.all_to_all(copies, WEIGHT_GROUP, 0, 0, tiled=True).reshape(QUAD, LANES)

    shifted = shift(signals, 1)
    blocks = call(
        split_kernel, [((OWN, 256), BF16)] * 4, [((QUAD, 256), BF16)], prm, shifted
    )
    blocks = [lax.ppermute(b, AX, pixel_pairs(v)) for v, b in enumerate(blocks)]
    x, a = call(start_kernel, [own, own], [], prm, *blocks)
    others = [turn_y(a, d) for d in (1, 2, 3)]
    g = swap(x, "xh")

    full, keep, send = call(
        first_kernel,
        [((QUAD, PIX), BF16), own32, own32],
        [((QUAD, LANES), BF16), ((LANES, PIX), BF16), ((PAIR, PIX), F32)],
        prm,
        w,
        a,
        *others,
        grant=24,
    )
    (mine,) = call(middle_kernel, [own], [], prm, x, keep, swap(send, "core"))
    theirs = swap(mine, "xh")
    b, q = call(turn_kernel, [own, own], [], prm, mine, theirs, g)
    b_other = swap(b, "core")
    (dw,) = call(
        weight_slope_kernel,
        [((QUAD, LANES), BF16)],
        [((PAIR, PIX), BF16), ((LANES, PIX), BF16)],
        prm,
        full,
        b,
        b_other,
        grant=24,
    )
    keep, *sends = call(
        second_kernel,
        [own32, own, own, own],
        [
            ((QUAD, LANES), BF16),
            ((PAIR, PIX), BF16),
            ((LANES, PIX), BF16),
            ((QUAD, PIX), F32),
        ],
        prm,
        w,
        b,
        b_other,
        grant=24,
    )
    got = [turn_y(s, d) for d, s in enumerate(sends, 1)]
    blocks = call(last_kernel, [((OWN, 256), BF16)] * 4, [own], prm, x, q, keep, *got)
    blocks = [lax.ppermute(b, AX, back(pixel_pairs(v))) for v, b in enumerate(blocks)]
    (joined,) = call(
        join_kernel, [((256, QUAD), BF16)], [((QUAD, 256), BF16)], prm, *blocks
    )
    results = shift(joined, -1)

    shares = lax.all_to_all(dw.reshape(16, 24, LANES), WEIGHT_GROUP, 0, 0, tiled=True)
    total = jnp.sum(shares.astype(F32), axis=0).astype(BF16)
    pieces = [jnp.where(flip, total[12:], total[:12]), jnp.where(flip, total[:12], total[12:])]
    low_high = [
        lax.ppermute(pieces[0], AX, back(weight_pairs(0))),
        lax.ppermute(pieces[1], AX, back(weight_pairs(1))),
    ]
    low = jnp.where(odd, low_high[1], low_high[0]).reshape(12, TAPS, 2, OWN)
    high = jnp.where(odd, low_high[0], low_high[1]).reshape(12, TAPS, 2, OWN)
    apart = jnp.concatenate([low, high], axis=2)
    woven = jnp.stack([low, high], axis=3).reshape(12, TAPS, 4, OWN)
    grad_weight = jnp.where(xh == 0, apart, woven).reshape(12, TAPS, QUAD).astype(F32)
    return results, grad_weight


def solution(mesh):
    finer = Mesh(mesh.devices.reshape(SIZES), AX)
    section, fsdp = ("xh", "core"), ("z", "xl", "y")
    placed = (P(fsdp, section), P(fsdp, None, section), P())
    return jax.shard_map(
        step,
        mesh=finer,
        in_specs=placed,
        out_specs=(P(fsdp, section), P(fsdp, None, section)),
        check_vma=False,
    )
```

```python
import jax
import jax.numpy as jnp
from jax import lax
from jax.experimental import pallas as pl
from jax.experimental.pallas import tpu as pltpu
from jax.sharding import Mesh
from jax.sharding import PartitionSpec as P


AX = ("xh", "core", "z", "xl", "y")
SIZES = (2, 2, 8, 2, 4)
WEIGHT_GROUP = ("z", "xl")
FSDP = ("z", "xl", "y")
GROUP_WIDTH = 24
OWN = 96
PIX = 1024
SIDE = 32
TAPS = 9
PAIR = 2 * OWN
QUAD = 4 * OWN
LANES = TAPS * PAIR
EPS = 1e-05
F32 = jnp.float32
BF16 = jnp.bfloat16


def flat(xh, core, z, xl, y):
    return (((xh * 2 + core) * 8 + z) * 2 + xl) * 4 + y


def every():
    for xh in range(2):
        for core in range(2):
            for z in range(8):
                for xl in range(2):
                    for y in range(4):
                        yield xh, core, z, xl, y


def pixel_pairs(turn, ahead):
    pairs = []
    for xh, core, z, xl, y in every():
        slot = ((z * 2 + xl) * 4 + y + ahead) % 64
        sample, piece = slot // 4, slot % 4
        u = (piece + turn) % 4
        pairs.append(
            (flat(xh, core, z, xl, y), flat(xh, u % 2, sample // 2, sample % 2, 2 * core + u // 2))
        )
    return pairs


def weight_pairs(second):
    pairs = []
    for xh, core, z, xl, y in every():
        b = (y & 1) ^ second
        if xh == 0:
            target = (0, z % 2, 2 * (z // 2) + xl, y >> 1, 2 * core + b)
        else:
            far = 2 * core + (y >> 1)
            target = (1, b, (z + (far if z % 2 else -far)) % 8, xl, z // 2)
        pairs.append((flat(xh, core, z, xl, y), flat(*target)))
    return pairs


def back(pairs):
    return [(b, a) for a, b in pairs]


def swap(value, axis):
    return lax.ppermute(value, axis, [(0, 1), (1, 0)])


def turn_y(value, d):
    return lax.ppermute(value, "y", [(i, (i + d) % 4) for i in range(4)])


def pixels():
    p = lax.broadcasted_iota(jnp.int32, (1, PIX), 1)
    return p >> 5, p & 31


def live(prm):
    row, col = pixels()
    return ((row < prm[3]) & (col < prm[4])).astype(F32)


def offsets(tap):
    return tap // 3 - 1, tap % 3 - 1


def moved(field, dr, dc):
    off = dr * SIDE + dc
    if off == 0:
        return field
    row, col = pixels()
    ok = (row + dr >= 0) & (row + dr < SIDE) & (col + dc >= 0) & (col + dc < SIDE)
    return pltpu.roll(field, (-off) % PIX, 1) * ok.astype(F32).astype(field.dtype)


def group_sum(field):
    return jnp.sum(field.reshape(OWN // GROUP_WIDTH, GROUP_WIDTH, PIX), axis=(1, 2), keepdims=True)


def spread(stat):
    return jnp.broadcast_to(stat, (OWN // GROUP_WIDTH, GROUP_WIDTH, PIX)).reshape(OWN, PIX)


def normed_of(values, mask, count):
    masked = values * mask
    mean = group_sum(masked) / count
    var = group_sum(masked * masked) / count - mean * mean
    scale = spread(lax.rsqrt(var + EPS))
    return (values - spread(mean)) * scale, scale


def count_of(prm):
    return (prm[3] * prm[4] * GROUP_WIDTH).astype(F32)


def silu_slope(u, s):
    return s * (1.0 + u * (1.0 - s))


def input_slope(e, xhat, scale, mask, count):
    m1 = spread(group_sum(e) / count)
    m2 = spread(group_sum(e * xhat) / count)
    return mask * (e - m1 - xhat * m2) * scale


def rows(k, n=OWN):
    return pl.ds(pl.multiple_of(k * n, n), n)


def split_kernel(prm, x_ref, *refs):
    outs, scratch = refs[:4], refs[4]
    scratch[...] = x_ref[...].astype(F32).T.astype(BF16)
    for v in range(4):
        outs[v][...] = scratch[rows((prm[2] + v) % 4), :]


def join_kernel(prm, *refs):
    ins, out, scratch = refs[:4], refs[4], refs[5]
    for v in range(4):
        scratch[rows((prm[5] + v) % 4), :] = ins[v][...]
    out[...] = scratch[...].astype(F32).T.astype(BF16)


def start_kernel(prm, *refs):
    ins, x_out, a_out = refs[:4], refs[4], refs[5]
    u = 2 * (prm[2] % 2) + prm[1]
    for v in range(4):
        t = (u - v + 4) % 4
        x_out[:, pl.ds(pl.multiple_of(t * 256, 256), 256)] = ins[v][...]
    mask = live(prm)
    values = x_out[...].astype(F32) * mask
    xhat, _ = normed_of(values, mask, count_of(prm))
    act = mask * (xhat * jax.nn.sigmoid(xhat))
    a_out[...] = jnp.where(prm[0] == 0, act, values).astype(BF16)


def convolve(w, act):
    acc = jnp.zeros((PAIR, PIX), F32)
    for tap in range(0, TAPS, 2):
        n = min(2, TAPS - tap)
        part = lax.dot_general(
            w[:, tap * PAIR : (tap + n) * PAIR],
            act,
            (((0,), (0,)), ((), ())),
            preferred_element_type=F32,
        )
        for k in range(n):
            acc = acc + moved(part[k * PAIR : (k + 1) * PAIR], *offsets(tap + k))
    return acc


def build_moved(act, d_ref):
    for tap in range(TAPS):
        dr, dc = offsets(tap)
        d_ref[tap * PAIR : (tap + 1) * PAIR, :] = moved(act, -dr, -dc)


def gather_chunks(prm, own, others, full):
    full[rows(prm[2]), :] = own[...]
    for d, ref in enumerate(others, 1):
        full[rows((prm[2] + 4 - d) % 4), :] = ref[...]


def parts_in_order(prm):
    for k in range(16):
        far, odd, xl = 2 * (k >> 3) + (k & 1), (k >> 2) & 1, (k >> 1) & 1
        plane = (2 * prm[2] + (1 + far if odd else 8 - far)) % 8
        yield k, rows(2 * plane + xl, 24)


def first_kernel(prm, w, a0, a1, a2, a3, full, keep, send, sorted_w, d_ref, res):
    gather_chunks(prm, a0, (a1, a2, a3), full)

    @pl.when(prm[0] == 0)
    def _():
        res[...] = convolve(w[...], full[...])

    @pl.when(prm[0] == 1)
    def _():
        for k, place in parts_in_order(prm):
            sorted_w[k * 24 : (k + 1) * 24, :] = w[place, :]
        for k in range(2):
            build_moved(full[k * PAIR : (k + 1) * PAIR, :], d_ref)
            part = jnp.dot(
                sorted_w[k * PAIR : (k + 1) * PAIR, :], d_ref[...], preferred_element_type=F32
            )
            if k == 0:
                res[...] = part
            else:
                res[...] += part

    keep[...] = res[rows(prm[1]), :]
    send[...] = res[rows(1 - prm[1]), :]


def middle_kernel(prm, x, keep, got, out):
    mask = live(prm)
    total = keep[...] + got[...]
    values = x[...].astype(F32) * mask
    out[...] = jnp.where(prm[0] == 0, values + mask * total, total).astype(BF16)


def turn_kernel(prm, mine, theirs, g, b_out, q_out):
    mask = live(prm)
    count = count_of(prm)
    down = prm[0] == 0
    hidden = jnp.where(down, mine[...].astype(F32), theirs[...].astype(F32))
    xhat, scale = normed_of(hidden, mask, count)
    s = jax.nn.sigmoid(xhat)

    @pl.when(down)
    def _():
        e = mask * theirs[...].astype(F32) * silu_slope(xhat, s)
        dv = (g[...].astype(F32) + input_slope(e, xhat, scale, mask, count)).astype(BF16)
        q_out[...] = dv
        b_out[...] = (dv.astype(F32) * mask).astype(BF16)

    @pl.when(jnp.logical_not(down))
    def _():
        q_out[...] = theirs[...]
        b_out[...] = (mask * (xhat * s)).astype(BF16)


def pair_up(prm, own, other, pair):
    pair[rows(prm[1]), :] = own[...]
    pair[rows(1 - prm[1]), :] = other[...]


def weight_slope_kernel(prm, full, b_own, b_other, dw, pair, d_ref):
    pair_up(prm, b_own, b_other, pair)

    def product(lhs):
        return lax.dot_general(
            lhs, d_ref[...], (((1,), (1,)), ((), ())), preferred_element_type=F32
        )

    @pl.when(prm[0] == 0)
    def _():
        build_moved(pair[...], d_ref)
        dw[...] = product(full[...]).astype(BF16)

    @pl.when(prm[0] == 1)
    def _():
        for k in range(2):
            build_moved(full[k * PAIR : (k + 1) * PAIR, :], d_ref)
            part = product(pair[...])
            for m, place in parts_in_order(prm):
                if m // 8 == k:
                    dw[place, :] = part[m % 8 * 24 : (m % 8 + 1) * 24, :].astype(BF16)


def second_kernel(prm, w, b_own, b_other, keep, s1, s2, s3, sorted_w, pair, d_ref, res):
    pair_up(prm, b_own, b_other, pair)

    @pl.when(prm[0] == 0)
    def _():
        build_moved(pair[...], d_ref)
        res[...] = jnp.dot(w[...], d_ref[...], preferred_element_type=F32)

    @pl.when(prm[0] == 1)
    def _():
        for k, place in parts_in_order(prm):
            sorted_w[k * 24 : (k + 1) * 24, :] = w[place, :]
        for k in range(2):
            res[k * PAIR : (k + 1) * PAIR, :] = convolve(
                sorted_w[k * PAIR : (k + 1) * PAIR, :], pair[...]
            )

    keep[...] = res[rows(prm[2]), :]
    for d, ref in enumerate((s1, s2, s3), 1):
        ref[...] = res[rows((prm[2] + d) % 4), :].astype(BF16)


def last_kernel(prm, x, q, keep, r1, r2, r3, *refs):
    outs, scratch = refs[:4], refs[4]
    mask = live(prm)
    count = count_of(prm)
    total = keep[...] + r1[...].astype(F32) + r2[...].astype(F32) + r3[...].astype(F32)
    carried = q[...].astype(F32)

    @pl.when(prm[0] == 0)
    def _():
        xhat, scale = normed_of(x[...].astype(F32) * mask, mask, count)
        e = mask * total * silu_slope(xhat, jax.nn.sigmoid(xhat))
        slope = input_slope(e, xhat, scale, mask, count)
        scratch[...] = (mask * (carried + slope)).astype(BF16)

    @pl.when(prm[0] == 1)
    def _():
        scratch[...] = (carried + mask * total).astype(BF16)

    u = 2 * (prm[2] % 2) + prm[1]
    for v in range(4):
        t = (u - v + 4) % 4
        outs[v][...] = scratch[:, pl.ds(pl.multiple_of(t * 256, 256), 256)]


def call(kernel, outs, scratch, prm, *args, grant=8):
    vmem = pl.BlockSpec(memory_space=pltpu.VMEM)
    return pl.pallas_call(
        kernel,
        out_shape=[jax.ShapeDtypeStruct(s, d) for s, d in outs],
        in_specs=[pl.BlockSpec(memory_space=pltpu.SMEM)] + [vmem] * len(args),
        out_specs=[vmem] * len(outs),
        scratch_shapes=[pltpu.VMEM(s, d) for s, d in scratch],
        compiler_params=pltpu.CompilerParams(vmem_limit_bytes=grant << 20),
    )(prm, *args)


def step(signals, conv_weight, buckets):
    xh, core, z, _, y = (lax.axis_index(a) for a in AX)
    micro = z // 4
    own_bucket = jnp.where(micro == 0, buckets[0], buckets[1])
    size = 16 + 2 * own_bucket
    piece = (y + 1) % 4
    prm = jnp.stack([xh, core, y, size[0], size[1], piece]).astype(jnp.int32)
    own = ((OWN, PIX), BF16)
    own32 = ((OWN, PIX), F32)

    cut = conv_weight.reshape(12, TAPS, 4, OWN)
    inner = [
        jnp.where(xh == 0, cut[:, :, 1:2], cut[:, :, 2:3]),
        jnp.where(xh == 0, cut[:, :, 2:3], cut[:, :, 1:2]),
    ]
    low = jnp.concatenate([cut[:, :, 0:1], inner[0]], axis=2).reshape(12, LANES)
    high = jnp.concatenate([inner[1], cut[:, :, 3:4]], axis=2).reshape(12, LANES)
    odd = y % 2 == 1
    got = [
        lax.ppermute(jnp.where(odd, high, low), AX, weight_pairs(0)),
        lax.ppermute(jnp.where(odd, low, high), AX, weight_pairs(1)),
    ]
    flip = jnp.where(xh == 0, y % 2, core) == 1
    part = jnp.concatenate([jnp.where(flip, got[1], got[0]), jnp.where(flip, got[0], got[1])], 0)
    copies = jnp.broadcast_to(part, (16, 24, LANES))
    w = lax.all_to_all(copies, WEIGHT_GROUP, 0, 0, tiled=True).reshape(QUAD, LANES)

    shifted = lax.ppermute(signals, FSDP, [(i, (i + 1) % 64) for i in range(64)])
    blocks = call(
        split_kernel, [((OWN, 256), BF16)] * 4, [((QUAD, 256), BF16)], prm, shifted
    )
    blocks = [lax.ppermute(b, AX, pixel_pairs(v, 0)) for v, b in enumerate(blocks)]
    x, a = call(start_kernel, [own, own], [], prm, *blocks)
    others = [turn_y(a, d) for d in (1, 2, 3)]
    g = swap(x, "xh")

    full, keep, send = call(
        first_kernel,
        [((QUAD, PIX), BF16), own32, own32],
        [((QUAD, LANES), BF16), ((LANES, PIX), BF16), ((PAIR, PIX), F32)],
        prm,
        w,
        a,
        *others,
        grant=24,
    )
    (mine,) = call(middle_kernel, [own], [], prm, x, keep, swap(send, "core"))
    theirs = swap(mine, "xh")
    b, q = call(turn_kernel, [own, own], [], prm, mine, theirs, g)
    b_other = swap(b, "core")
    (dw,) = call(
        weight_slope_kernel,
        [((QUAD, LANES), BF16)],
        [((PAIR, PIX), BF16), ((LANES, PIX), BF16)],
        prm,
        full,
        b,
        b_other,
        grant=24,
    )
    keep, *sends = call(
        second_kernel,
        [own32, own, own, own],
        [
            ((QUAD, LANES), BF16),
            ((PAIR, PIX), BF16),
            ((LANES, PIX), BF16),
            ((QUAD, PIX), F32),
        ],
        prm,
        w,
        b,
        b_other,
        grant=24,
    )
    got = [turn_y(s, d) for d, s in enumerate(sends, 1)]
    blocks = call(last_kernel, [((OWN, 256), BF16)] * 4, [own], prm, x, q, keep, *got)
    blocks = [lax.ppermute(b, AX, back(pixel_pairs(v, 1))) for v, b in enumerate(blocks)]
    (results,) = call(
        join_kernel, [((256, QUAD), BF16)], [((QUAD, 256), BF16)], prm, *blocks
    )

    shares = lax.all_to_all(dw.reshape(16, 24, LANES), WEIGHT_GROUP, 0, 0, tiled=True)
    total = shares[0].astype(F32)
    for k in range(1, 16):
        total = total + shares[k].astype(F32)
    total = total.astype(BF16)
    first, second = total[:12], total[12:]
    low_high = [
        lax.ppermute(jnp.where(flip, second, first), AX, back(weight_pairs(0))),
        lax.ppermute(jnp.where(flip, first, second), AX, back(weight_pairs(1))),
    ]
    low = jnp.where(odd, low_high[1], low_high[0]).reshape(12, TAPS, 2, OWN)
    high = jnp.where(odd, low_high[0], low_high[1]).reshape(12, TAPS, 2, OWN)
    inner = [
        jnp.where(xh == 0, low[:, :, 1:2], high[:, :, 0:1]),
        jnp.where(xh == 0, high[:, :, 0:1], low[:, :, 1:2]),
    ]
    chunks = [low[:, :, 0:1], inner[0], inner[1], high[:, :, 1:2]]
    grad_weight = jnp.concatenate(chunks, axis=2).reshape(12, TAPS, QUAD).astype(F32)
    return results, grad_weight


def solution(mesh):
    finer = Mesh(mesh.devices.reshape(SIZES), AX)
    section, fsdp = ("xh", "core"), ("z", "xl", "y")
    placed = (P(fsdp, section), P(fsdp, None, section), P())
    return jax.shard_map(
        step,
        mesh=finer,
        in_specs=placed,
        out_specs=(P(fsdp, section), P(fsdp, None, section)),
        check_vma=False,
    )
```

```python
import jax
import jax.numpy as jnp
from jax import lax
from jax.experimental import pallas as pl
from jax.experimental.pallas import tpu as pltpu
from jax.sharding import Mesh
from jax.sharding import PartitionSpec as P


AX = ("xh", "core", "z", "xl", "y")
SIZES = (2, 2, 8, 2, 4)
WEIGHT_GROUP = ("z", "xl")
FSDP = ("z", "xl", "y")
GROUP_WIDTH = 24
OWN = 96
PIX = 1024
SIDE = 32
TAPS = 9
PAIR = 2 * OWN
QUAD = 4 * OWN
LANES = TAPS * PAIR
EPS = 1e-05
F32 = jnp.float32
BF16 = jnp.bfloat16


def flat(xh, core, z, xl, y):
    return (((xh * 2 + core) * 8 + z) * 2 + xl) * 4 + y


def every():
    for xh in range(2):
        for core in range(2):
            for z in range(8):
                for xl in range(2):
                    for y in range(4):
                        yield xh, core, z, xl, y


def pixel_pairs(turn, ahead):
    pairs = []
    for xh, core, z, xl, y in every():
        slot = ((z * 2 + xl) * 4 + y + ahead) % 64
        sample, piece = slot // 4, slot % 4
        u = (piece + turn) % 4
        pairs.append(
            (flat(xh, core, z, xl, y), flat(xh, u % 2, sample // 2, sample % 2, 2 * core + u // 2))
        )
    return pairs


def weight_pairs(second):
    pairs = []
    for xh, core, z, xl, y in every():
        b = (y & 1) ^ second
        if xh == 0:
            target = (0, z % 2, 2 * (z // 2) + xl, y >> 1, 2 * core + b)
        else:
            far = 2 * core + (y >> 1)
            target = (1, b, (z + (far if z % 2 else -far)) % 8, xl, z // 2)
        pairs.append((flat(xh, core, z, xl, y), flat(*target)))
    return pairs


def back(pairs):
    return [(b, a) for a, b in pairs]


def swap(value, axis):
    return lax.ppermute(value, axis, [(0, 1), (1, 0)])


def turn_y(value, d):
    return lax.ppermute(value, "y", [(i, (i + d) % 4) for i in range(4)])


def pixels():
    p = lax.broadcasted_iota(jnp.int32, (1, PIX), 1)
    return p >> 5, p & 31


def live(prm):
    row, col = pixels()
    return ((row < prm[3]) & (col < prm[4])).astype(F32)


def offsets(tap):
    return tap // 3 - 1, tap % 3 - 1


def moved(field, dr, dc):
    off = dr * SIDE + dc
    if off == 0:
        return field
    row, col = pixels()
    ok = (row + dr >= 0) & (row + dr < SIDE) & (col + dc >= 0) & (col + dc < SIDE)
    return pltpu.roll(field, (-off) % PIX, 1) * ok.astype(F32).astype(field.dtype)


def group_sum(field):
    return jnp.sum(field.reshape(OWN // GROUP_WIDTH, GROUP_WIDTH, PIX), axis=(1, 2), keepdims=True)


def spread(stat):
    return jnp.broadcast_to(stat, (OWN // GROUP_WIDTH, GROUP_WIDTH, PIX)).reshape(OWN, PIX)


def normed_of(values, mask, count):
    masked = values * mask
    mean = group_sum(masked) / count
    var = group_sum(masked * masked) / count - mean * mean
    scale = spread(lax.rsqrt(var + EPS))
    return (values - spread(mean)) * scale, scale


def count_of(prm):
    return (prm[3] * prm[4] * GROUP_WIDTH).astype(F32)


def silu_slope(u, s):
    return s * (1.0 + u * (1.0 - s))


def input_slope(e, xhat, scale, mask, count):
    m1 = spread(group_sum(e) / count)
    m2 = spread(group_sum(e * xhat) / count)
    return mask * (e - m1 - xhat * m2) * scale


def rows(k, n=OWN):
    return pl.ds(pl.multiple_of(k * n, n), n)


def split_kernel(prm, x_ref, *refs):
    outs, scratch = refs[:4], refs[4]
    scratch[...] = x_ref[...].astype(F32).T.astype(BF16)
    for v in range(4):
        outs[v][...] = scratch[rows((prm[2] + v) % 4), :]


def join_kernel(prm, *refs):
    ins, out, scratch = refs[:4], refs[4], refs[5]
    for v in range(4):
        scratch[rows((prm[5] + v) % 4), :] = ins[v][...]
    out[...] = scratch[...].astype(F32).T.astype(BF16)


def start_kernel(prm, *refs):
    ins, x_out, a_out = refs[:4], refs[4], refs[5]
    u = 2 * (prm[2] % 2) + prm[1]
    for v in range(4):
        t = (u - v + 4) % 4
        x_out[:, pl.ds(pl.multiple_of(t * 256, 256), 256)] = ins[v][...]
    mask = live(prm)
    values = x_out[...].astype(F32) * mask
    xhat, _ = normed_of(values, mask, count_of(prm))
    act = mask * (xhat * jax.nn.sigmoid(xhat))
    a_out[...] = jnp.where(prm[0] == 0, act, values).astype(BF16)


def convolve(w, act):
    acc = jnp.zeros((PAIR, PIX), F32)
    for tap in range(0, TAPS, 2):
        n = min(2, TAPS - tap)
        part = lax.dot_general(
            w[:, tap * PAIR : (tap + n) * PAIR],
            act,
            (((0,), (0,)), ((), ())),
            preferred_element_type=F32,
        )
        for k in range(n):
            acc = acc + moved(part[k * PAIR : (k + 1) * PAIR], *offsets(tap + k))
    return acc


def build_moved(act, d_ref):
    for tap in range(TAPS):
        dr, dc = offsets(tap)
        d_ref[tap * PAIR : (tap + 1) * PAIR, :] = moved(act, -dr, -dc)


def gather_chunks(prm, own, others, full):
    full[rows(prm[2]), :] = own[...]
    for d, ref in enumerate(others, 1):
        full[rows((prm[2] + 4 - d) % 4), :] = ref[...]


def parts_in_order(prm):
    for k in range(16):
        far, odd, xl = 2 * (k >> 3) + (k & 1), (k >> 2) & 1, (k >> 1) & 1
        plane = (2 * prm[2] + (1 + far if odd else 8 - far)) % 8
        yield k, rows(2 * plane + xl, 24)


def first_kernel(prm, w, a0, a1, a2, a3, full, keep, send, sorted_w, d_ref, res):
    gather_chunks(prm, a0, (a1, a2, a3), full)

    @pl.when(prm[0] == 0)
    def _():
        res[...] = convolve(w[...], full[...])

    @pl.when(prm[0] == 1)
    def _():
        for k, place in parts_in_order(prm):
            sorted_w[k * 24 : (k + 1) * 24, :] = w[place, :]
        for k in range(2):
            build_moved(full[k * PAIR : (k + 1) * PAIR, :], d_ref)
            part = jnp.dot(
                sorted_w[k * PAIR : (k + 1) * PAIR, :], d_ref[...], preferred_element_type=F32
            )
            if k == 0:
                res[...] = part
            else:
                res[...] += part

    keep[...] = res[rows(prm[1]), :]
    send[...] = res[rows(1 - prm[1]), :]


def middle_kernel(prm, x, keep, got, out):
    mask = live(prm)
    total = keep[...] + got[...]
    values = x[...].astype(F32) * mask
    out[...] = jnp.where(prm[0] == 0, values + mask * total, total).astype(BF16)


def turn_kernel(prm, mine, theirs, g, b_out, q_out):
    mask = live(prm)
    count = count_of(prm)
    down = prm[0] == 0
    hidden = jnp.where(down, mine[...].astype(F32), theirs[...].astype(F32))
    xhat, scale = normed_of(hidden, mask, count)
    s = jax.nn.sigmoid(xhat)

    @pl.when(down)
    def _():
        e = mask * theirs[...].astype(F32) * silu_slope(xhat, s)
        dv = (g[...].astype(F32) + input_slope(e, xhat, scale, mask, count)).astype(BF16)
        q_out[...] = dv
        b_out[...] = (dv.astype(F32) * mask).astype(BF16)

    @pl.when(jnp.logical_not(down))
    def _():
        q_out[...] = theirs[...]
        b_out[...] = (mask * (xhat * s)).astype(BF16)


def pair_up(prm, own, other, pair):
    pair[rows(prm[1]), :] = own[...]
    pair[rows(1 - prm[1]), :] = other[...]


def weight_slope_kernel(prm, full, b_own, b_other, dw, pair, d_ref):
    pair_up(prm, b_own, b_other, pair)

    def product(lhs):
        return lax.dot_general(
            lhs, d_ref[...], (((1,), (1,)), ((), ())), preferred_element_type=F32
        )

    @pl.when(prm[0] == 0)
    def _():
        build_moved(pair[...], d_ref)
        dw[...] = product(full[...]).astype(BF16)

    @pl.when(prm[0] == 1)
    def _():
        for k in range(2):
            build_moved(full[k * PAIR : (k + 1) * PAIR, :], d_ref)
            part = product(pair[...])
            for m, place in parts_in_order(prm):
                if m // 8 == k:
                    dw[place, :] = part[m % 8 * 24 : (m % 8 + 1) * 24, :].astype(BF16)


def second_kernel(prm, w, b_own, b_other, keep, s1, s2, s3, sorted_w, pair, d_ref, res):
    pair_up(prm, b_own, b_other, pair)

    @pl.when(prm[0] == 0)
    def _():
        build_moved(pair[...], d_ref)
        res[...] = jnp.dot(w[...], d_ref[...], preferred_element_type=F32)

    @pl.when(prm[0] == 1)
    def _():
        for k, place in parts_in_order(prm):
            sorted_w[k * 24 : (k + 1) * 24, :] = w[place, :]
        for k in range(2):
            res[k * PAIR : (k + 1) * PAIR, :] = convolve(
                sorted_w[k * PAIR : (k + 1) * PAIR, :], pair[...]
            )

    keep[...] = res[rows(prm[2]), :]
    for d, ref in enumerate((s1, s2, s3), 1):
        ref[...] = res[rows((prm[2] + d) % 4), :].astype(BF16)


def last_kernel(prm, x, q, keep, r1, r2, r3, *refs):
    outs, scratch = refs[:4], refs[4]
    mask = live(prm)
    count = count_of(prm)
    total = keep[...] + r1[...].astype(F32) + r2[...].astype(F32) + r3[...].astype(F32)
    carried = q[...].astype(F32)

    @pl.when(prm[0] == 0)
    def _():
        xhat, scale = normed_of(x[...].astype(F32) * mask, mask, count)
        e = mask * total * silu_slope(xhat, jax.nn.sigmoid(xhat))
        slope = input_slope(e, xhat, scale, mask, count)
        scratch[...] = (mask * (carried + slope)).astype(BF16)

    @pl.when(prm[0] == 1)
    def _():
        scratch[...] = (carried + mask * total).astype(BF16)

    u = 2 * (prm[2] % 2) + prm[1]
    for v in range(4):
        t = (u - v + 4) % 4
        outs[v][...] = scratch[:, pl.ds(pl.multiple_of(t * 256, 256), 256)]


def call(kernel, outs, scratch, prm, *args, grant=8):
    vmem = pl.BlockSpec(memory_space=pltpu.VMEM)
    return pl.pallas_call(
        kernel,
        out_shape=[jax.ShapeDtypeStruct(s, d) for s, d in outs],
        in_specs=[pl.BlockSpec(memory_space=pltpu.SMEM)] + [vmem] * len(args),
        out_specs=[vmem] * len(outs),
        scratch_shapes=[pltpu.VMEM(s, d) for s, d in scratch],
        compiler_params=pltpu.CompilerParams(vmem_limit_bytes=grant << 20),
    )(prm, *args)


def step(signals, conv_weight, buckets):
    xh, core, z, _, y = (lax.axis_index(a) for a in AX)
    micro = z // 4
    own_bucket = jnp.where(micro == 0, buckets[0], buckets[1])
    size = 16 + 2 * own_bucket
    piece = (y + 1) % 4
    prm = jnp.stack([xh, core, y, size[0], size[1], piece]).astype(jnp.int32)
    own = ((OWN, PIX), BF16)
    own32 = ((OWN, PIX), F32)

    cut = [conv_weight[:, :, k * OWN : (k + 1) * OWN] for k in range(4)]
    inner = [jnp.where(xh == 0, cut[1], cut[2]), jnp.where(xh == 0, cut[2], cut[1])]
    low = jnp.concatenate([cut[0], inner[0]], axis=2).reshape(12, LANES)
    high = jnp.concatenate([inner[1], cut[3]], axis=2).reshape(12, LANES)
    odd = y % 2 == 1
    got = [
        lax.ppermute(jnp.where(odd, high, low), AX, weight_pairs(0)),
        lax.ppermute(jnp.where(odd, low, high), AX, weight_pairs(1)),
    ]
    flip = jnp.where(xh == 0, y % 2, core) == 1
    part = jnp.concatenate([jnp.where(flip, got[1], got[0]), jnp.where(flip, got[0], got[1])], 0)
    copies = jnp.broadcast_to(part, (16, 24, LANES))
    w = lax.all_to_all(copies, WEIGHT_GROUP, 0, 0, tiled=True).reshape(QUAD, LANES)

    shifted = lax.ppermute(signals, FSDP, [(i, (i + 1) % 64) for i in range(64)])
    blocks = call(
        split_kernel, [((OWN, 256), BF16)] * 4, [((QUAD, 256), BF16)], prm, shifted
    )
    blocks = [lax.ppermute(b, AX, pixel_pairs(v, 0)) for v, b in enumerate(blocks)]
    x, a = call(start_kernel, [own, own], [], prm, *blocks)
    others = [turn_y(a, d) for d in (1, 2, 3)]
    g = swap(x, "xh")

    full, keep, send = call(
        first_kernel,
        [((QUAD, PIX), BF16), own32, own32],
        [((QUAD, LANES), BF16), ((LANES, PIX), BF16), ((PAIR, PIX), F32)],
        prm,
        w,
        a,
        *others,
        grant=24,
    )
    (mine,) = call(middle_kernel, [own], [], prm, x, keep, swap(send, "core"))
    theirs = swap(mine, "xh")
    b, q = call(turn_kernel, [own, own], [], prm, mine, theirs, g)
    b_other = swap(b, "core")
    (dw,) = call(
        weight_slope_kernel,
        [((QUAD, LANES), BF16)],
        [((PAIR, PIX), BF16), ((LANES, PIX), BF16)],
        prm,
        full,
        b,
        b_other,
        grant=24,
    )
    keep, *sends = call(
        second_kernel,
        [own32, own, own, own],
        [
            ((QUAD, LANES), BF16),
            ((PAIR, PIX), BF16),
            ((LANES, PIX), BF16),
            ((QUAD, PIX), F32),
        ],
        prm,
        w,
        b,
        b_other,
        grant=24,
    )
    got = [turn_y(s, d) for d, s in enumerate(sends, 1)]
    blocks = call(last_kernel, [((OWN, 256), BF16)] * 4, [own], prm, x, q, keep, *got)
    blocks = [lax.ppermute(b, AX, back(pixel_pairs(v, 1))) for v, b in enumerate(blocks)]
    (results,) = call(
        join_kernel, [((256, QUAD), BF16)], [((QUAD, 256), BF16)], prm, *blocks
    )

    shares = lax.all_to_all(dw.reshape(16, 24, LANES), WEIGHT_GROUP, 0, 0, tiled=True)
    total = shares[0].astype(F32)
    for k in range(1, 16):
        total = total + shares[k].astype(F32)
    total = total.astype(BF16)
    first, second = total[:12], total[12:]
    low_high = [
        lax.ppermute(jnp.where(flip, second, first), AX, back(weight_pairs(0))),
        lax.ppermute(jnp.where(flip, first, second), AX, back(weight_pairs(1))),
    ]
    low = jnp.where(odd, low_high[1], low_high[0]).reshape(12, TAPS, PAIR)
    high = jnp.where(odd, low_high[0], low_high[1]).reshape(12, TAPS, PAIR)
    inner = [low[:, :, OWN:], high[:, :, :OWN]]
    chunks = [
        low[:, :, :OWN],
        jnp.where(xh == 0, inner[0], inner[1]),
        jnp.where(xh == 0, inner[1], inner[0]),
        high[:, :, OWN:],
    ]
    grad_weight = jnp.concatenate(chunks, axis=2).astype(F32)
    return results, grad_weight


def solution(mesh):
    finer = Mesh(mesh.devices.reshape(SIZES), AX)
    section, fsdp = ("xh", "core"), ("z", "xl", "y")
    placed = (P(fsdp, section), P(fsdp, None, section), P())
    return jax.shard_map(
        step,
        mesh=finer,
        in_specs=placed,
        out_specs=(P(fsdp, section), P(fsdp, None, section)),
        check_vma=False,
    )
```
